512 devices in a mesh: slab: 8 (over z), energy: 64 (over y, x, core).
Axes of the slice: x: 4, y: 8, z: 8, core: 2. Of those that a mesh axis runs over, the one named last changes fastest.
Arguments:
- retarded: float32 [8, 128, 2, 256, 256], P('slab', 'energy'), may hold values from -0.375 to 0.375
- lesser_prev: float32 [8, 128, 2, 256, 256], P('slab', 'energy'), may hold values from -1.8 to 1.8
- hopping: float32 [8, 256, 256], P('slab'), may hold values from -0.375 to 0.375
- hop_mask: int32 [8, 4, 4], P('slab'), may hold values 0 or 1
- offsets: int32 [3], replicated, may hold values from 1 to 6, as said below
- coupling: float32 [3], replicated, may hold values from 0.3 to 1
- occupation: float32 [3], replicated, may hold values from 0.1 to 3
Outputs:
- lesser: float32 [8, 128, 2, 256, 256], P('slab', 'energy')
The draws below stay inside these ranges and needn't reach their ends.
Inputs may be any that keep to these rules, and one draw needn't show every extreme that they name: `offsets`: the offset of mode k lies in k * 2 + 1 to (k + 1) * 2, and the last mode's equals 6.
All inputs are finite; a program needn't handle non-finite values. No bound on the sum of `hop_mask` on one device may be relied on, other than what follows from the above.
Results may differ from the reference program's by a relative error of at most 0.00014.
Values sent between devices are 32-bit elements; how exact they have to be, the bound alone decides.
A program may use at most 64 MiB of HBM per device.

```python
import math
import jax
import jax.numpy as jnp
from jax import lax

B = 256
TILE = 64
E_DEV = 2
MODES = 3
QMAX = 6
NE = 128
SLABS = 8


def draw_offsets(key, part):
    mode_index = jnp.arange(MODES, dtype=jnp.int32)
    jitter = jax.random.randint(key, (MODES,), 0, E_DEV, dtype=jnp.int32)
    drawn = mode_index * E_DEV + 1 + jitter
    return jnp.where(mode_index == MODES - 1, MODES * E_DEV, drawn).astype(jnp.int32)


def place_ends(entries, stream_key, low, largest):
    spot = [jax.random.randint(jax.random.fold_in(stream_key, axis), (), 0, length) for axis, length in enumerate(entries.shape)]
    main_axis = entries.shape.index(max(entries.shape))
    beside = spot[:main_axis] + [(spot[main_axis] + 1) % entries.shape[main_axis]] + spot[main_axis + 1:]
    return entries.at[tuple(spot)].set(low).at[tuple(beside)].set(largest)


def steps_of(rng, shape, pieces, smallest, high):
    def one(position, parts):
        steps = jax.random.uniform(jax.random.fold_in(jax.random.fold_in(rng, 6), position), (parts,), jnp.float32, smallest / len(pieces), high / len(pieces))
        return jnp.repeat(jnp.exp(steps), shape[position] // parts).reshape((-1,) + (1,) * (len(shape) - position - 1))

    loudness = one(*pieces[0])
    for cut in pieces[1:]:
        loudness = loudness * one(*cut)
    return loudness


def scatter_about(stream_key, dims, scale, most, shards=(), kind=jnp.bfloat16):
    entries = jax.random.normal(stream_key, dims, jnp.float32) * scale
    if len(shards) > 0:
        entries = steps_of(stream_key, dims, shards, -0.22, 0.18) * entries
    return jnp.clip(entries, min=-most, max=most).astype(kind)


def setup_inputs(seed: int = 0) -> dict:
    streams_of = jax.random.split(jax.random.key(seed), 8)
    retarded = scatter_about(streams_of[0], (SLABS, NE, 2, B, B), B ** -0.5, 0.375, ((0, 8), (1, 64)), jnp.float32)
    lesser_prev = scatter_about(streams_of[1], (SLABS, NE, 2, B, B), 0.3, 1.8, ((0, 8), (1, 64)), jnp.float32)
    hopping = scatter_about(streams_of[2], (SLABS, B, B), B ** -0.5, 0.375, ((0, 8),), jnp.float32)
    hop_mask = place_ends((jax.random.randint(streams_of[3], (SLABS, B // TILE, B // TILE), 0, 2) < 1).astype(jnp.int32), jax.random.fold_in(streams_of[3], 1), 0, 1)
    offsets = draw_offsets(jax.random.fold_in(streams_of[7], 71), 0)
    coupling = jnp.clip(jnp.exp(jax.random.uniform(streams_of[5], (MODES,), jnp.float32, math.log(0.3), math.log(1.0))), 0.3, 1.0)
    occupation = jnp.clip(jnp.exp(jax.random.uniform(streams_of[6], (MODES,), jnp.float32, math.log(0.1), math.log(3.0))), 0.1, 3.0)
    return dict(retarded=retarded, lesser_prev=lesser_prev, hopping=hopping, hop_mask=hop_mask, offsets=offsets, coupling=coupling, occupation=occupation)


def matmul_high(left_matrix, right_matrix):
    return jnp.einsum("...ij,...jk->...ik", left_matrix, right_matrix, precision=lax.Precision.HIGHEST, preferred_element_type=jnp.float32)


def matmul_transposed(left_matrix, right_matrix):
    return jnp.einsum("...ij,...kj->...ik", left_matrix, right_matrix, precision=lax.Precision.HIGHEST, preferred_element_type=jnp.float32)


def complex_product(left_factor, right_factor):
    left_real, left_imag = left_factor[..., 0, :, :], left_factor[..., 1, :, :]
    right_real, right_imag = right_factor[..., 0, :, :], right_factor[..., 1, :, :]
    real_part = matmul_high(left_real, right_real) - matmul_high(left_imag, right_imag)
    imag_part = matmul_high(left_real, right_imag) + matmul_high(left_imag, right_real)
    return jnp.stack([real_part, imag_part], axis=-3)


def product_adjoint(left_factor, right_factor):
    left_real, left_imag = left_factor[..., 0, :, :], left_factor[..., 1, :, :]
    right_real, right_imag = right_factor[..., 0, :, :], right_factor[..., 1, :, :]
    real_part = matmul_transposed(left_real, right_real) + matmul_transposed(left_imag, right_imag)
    imag_part = matmul_transposed(left_imag, right_real) - matmul_transposed(left_real, right_imag)
    return jnp.stack([real_part, imag_part], axis=-3)


def masked_hopping(hopping_block, mask_block, tile_size):
    blocks = mask_block.shape[-1]
    expanded = jnp.broadcast_to(mask_block.astype(jnp.float32)[:, None, :, None], (blocks, tile_size, blocks, tile_size))
    return hopping_block * expanded.reshape(blocks * tile_size, blocks * tile_size)


def reference(retarded, lesser_prev, hopping, hop_mask, offsets, coupling, occupation):
    offsets_int = offsets.astype(jnp.int32)
    energies = lesser_prev.shape[1]
    results = []
    current = None
    for slab_index in range(SLABS):
        padded = jnp.pad(lesser_prev[slab_index], ((QMAX, QMAX), (0, 0), (0, 0), (0, 0)))
        self_energy = jnp.zeros(lesser_prev[slab_index].shape, jnp.float32)
        for mode_index in range(MODES):
            start_upper = (QMAX + offsets_int[mode_index]).astype(jnp.int32)
            start_lower = (QMAX - offsets_int[mode_index]).astype(jnp.int32)
            upper_piece = lax.dynamic_slice_in_dim(padded, start_upper, energies, 0)
            lower_piece = lax.dynamic_slice_in_dim(padded, start_lower, energies, 0)
            self_energy = self_energy + coupling[mode_index] * ((occupation[mode_index] + 1.0) * upper_piece + occupation[mode_index] * lower_piece)
        source = product_adjoint(complex_product(retarded[slab_index], self_energy), retarded[slab_index])
        if slab_index == 0:
            current = source
        else:
            coupled = matmul_high(retarded[slab_index], masked_hopping(hopping[slab_index], hop_mask[slab_index], TILE))
            current = source + product_adjoint(complex_product(coupled, current), coupled)
        results.append(current)
    return jnp.stack(results)
```

```python
import jax
import jax.numpy as jnp
from jax import lax
from jax.experimental import pallas as pl
from jax.experimental.pallas import tpu as pltpu
from jax.sharding import PartitionSpec as P

MESH = pl.DeviceIdType.MESH
F32 = jnp.float32
BF16 = jnp.bfloat16


def split(value):
    high = value.astype(BF16)
    return high, (value - high.astype(F32)).astype(BF16)


def dot(left, right):
    return jnp.dot(left, right, preferred_element_type=F32)


def masked_hopping(hop_ref, mask_ref, size):
    tiles = mask_ref.shape[-1]
    tile = size // tiles
    column = lax.broadcasted_iota(jnp.int32, (tile, size), 1)
    rows = []
    for i in range(tiles):
        keep = jnp.full((tile, size), mask_ref[0, i, tiles - 1].astype(F32))
        for j in range(tiles - 2, -1, -1):
            keep = jnp.where(column < (j + 1) * tile, mask_ref[0, i, j].astype(F32), keep)
        rows.append(hop_ref[i * tile : (i + 1) * tile, :] * keep)
    return jnp.concatenate(rows, axis=0)


def prepare(right_ref, left_ref, slot, real, imag):
    size = real.shape[0]
    half = size // 2
    for source, places in ((real, 0), (imag, 1)):
        high, low = split(source.T)
        for part, starts in ((high, (0, 4 * size)), (low, (2 * size,))):
            for start in starts:
                if places == 0:
                    right_ref[slot, start : start + size, 0:size] = part
                    right_ref[slot, start + size : start + 2 * size, size : 2 * size] = part
                else:
                    right_ref[slot, start : start + size, size : 2 * size] = -part
                    right_ref[slot, start + size : start + 2 * size, 0:size] = part
        high, low = split(source)
        for part, starts in ((high, (0, 2 * half)), (low, (4 * half,))):
            for g in range(2):
                for h in range(2):
                    block = part[g * half : (g + 1) * half, h * half : (h + 1) * half]
                    for start in starts:
                        if places == 0:
                            left_ref[slot, g, h, 0:half, start : start + half] = block
                            left_ref[slot, g, h, half : 2 * half, start + half : start + 2 * half] = block
                        else:
                            left_ref[slot, g, h, 0:half, start + half : start + 2 * half] = -block
                            left_ref[slot, g, h, half : 2 * half, start : start + half] = block


def half_times_adjoint(right_ref, slot, middle):
    size = middle.shape[-1]
    real_high, real_low = split(middle[0])
    imag_high, imag_low = split(middle[1])
    left = jnp.concatenate([real_high, imag_high, real_high, imag_high, real_low, imag_low], axis=1)
    product = dot(left, right_ref[slot])
    stacked = jnp.concatenate([product[:, 0:size], product[:, size : 2 * size]], axis=0)
    high, low = split(stacked)
    return jnp.concatenate([high, low, high], axis=0)


def kernel(
    retarded_hbm, lesser_hbm, hop_hbm, mask_ref, offsets_ref, coupling_ref, occupation_ref,
    out_hbm,
    held, partial_out, partial_in, retarded, hop, incoming, result, right_ref, left_ref,
    load_sem, near_send, near_recv, part_send, part_recv, chain_send, chain_recv, out_sem, gate,
):
    slab = lax.axis_index("slab")
    slabs = lax.axis_size("slab")
    place = lax.axis_index("energy")
    places = lax.axis_size("energy")
    core = lax.rem(place, 2)
    sign = 2 * core - 1
    size = retarded.shape[-1]
    half = size // 2

    def ring(index):
        return lax.rem(index + places, places)

    partner = place - sign
    across = ring(place + sign)
    ahead = ring(place + 2 * sign)
    behind = ring(place - 2 * sign)
    up = lax.rem(slab + 1, slabs)
    down = lax.rem(slab + slabs - 1, slabs)

    loads = [
        pltpu.make_async_copy(lesser_hbm.at[0], held.at[0], load_sem.at[0]),
        pltpu.make_async_copy(retarded_hbm.at[0], retarded, load_sem.at[1]),
        pltpu.make_async_copy(hop_hbm.at[0], hop, load_sem.at[2]),
    ]
    for load in loads:
        load.start()

    barrier = pltpu.get_barrier_semaphore()
    for other in (partner, across, ahead, behind):
        pl.semaphore_signal(barrier, inc=1, device_id={"slab": slab, "energy": other}, device_id_type=MESH)
    for other in (up, down):
        pl.semaphore_signal(barrier, inc=1, device_id={"slab": other, "energy": place}, device_id_type=MESH)
    pl.semaphore_wait(barrier, 6)

    def near_copy(slot, other):
        return pltpu.make_async_remote_copy(
            src_ref=lesser_hbm.at[0], dst_ref=held.at[slot],
            send_sem=near_send.at[slot - 1], recv_sem=near_recv.at[slot - 1],
            device_id={"slab": slab, "energy": other}, device_id_type=MESH,
        )

    to_partner = near_copy(1, partner)
    to_across = near_copy(2, across)
    to_partner.start()
    to_across.start()

    def part_copy(role, u):
        other = ahead if role == 0 else behind
        return pltpu.make_async_remote_copy(
            src_ref=partial_out.at[role, u], dst_ref=partial_in.at[role, u],
            send_sem=part_send.at[role, u], recv_sem=part_recv.at[role, u],
            device_id={"slab": slab, "energy": other}, device_id_type=MESH,
        )

    def chain_copy(u, g):
        rows = pl.ds(g * half, half)
        return pltpu.make_async_remote_copy(
            src_ref=result.at[u, :, rows, :], dst_ref=incoming.at[u, :, rows, :],
            send_sem=chain_send.at[u, g], recv_sem=chain_recv.at[u, g],
            device_id={"slab": up, "energy": place}, device_id_type=MESH,
        )

    modes = offsets_ref.shape[0]
    steps = [offsets_ref[k] for k in range(modes)]
    absorb = [coupling_ref[k] * occupation_ref[k] for k in range(modes)]
    emit = [coupling_ref[k] * (occupation_ref[k] + 1.0) for k in range(modes)]

    def weight(distance, above):
        total = jnp.float32(0.0)
        for k in range(modes):
            factor = jnp.where(above == 1, emit[k], absorb[k])
            total = total + jnp.where(steps[k] == distance, factor, 0.0)
        return total

    def inside(index):
        return jnp.where((index >= 0) & (index < places), 1.0, 0.0).astype(F32)

    loads[1].wait()
    loads[2].wait()
    mask_high, mask_low = split(masked_hopping(hop, mask_ref, size))
    hopping = jnp.concatenate([mask_high, mask_low, mask_high], axis=0)

    def operands(u, carry):
        real, imag = retarded[u, 0], retarded[u, 1]
        prepare(right_ref, left_ref, u, real, imag)
        high, low = split(jnp.concatenate([real, imag], axis=0))
        coupled = dot(jnp.concatenate([high, high, low], axis=1), hopping)
        prepare(right_ref, left_ref, 2 + u, coupled[0:size], coupled[size : 2 * size])
        return carry

    loads[0].wait()
    to_partner.wait()
    above_ahead = 1 - core
    above_behind = core
    for u in range(2):
        total = None
        for slot, reach in ((0, 4), (1, 6)):
            for b in range(2):
                term = weight(reach + sign * (u - b), above_ahead) * held[slot, b]
                total = term if total is None else total + term
        partial_out[0, u] = total

    @pl.when(core == 0)
    def _():
        for u in range(2):
            part_copy(0, u).start()

    lax.fori_loop(0, 2, operands, 0)

    to_across.wait()
    across_valid = inside(place + sign)
    for u in range(2):
        total = None
        for slot, reach in ((0, 4), (1, 2), (2, 6)):
            for b in range(2):
                factor = weight(reach - sign * (u - b), above_behind)
                if slot == 2:
                    factor = factor * across_valid
                term = factor * held[slot, b]
                total = term if total is None else total + term
        partial_out[1, u] = total

        @pl.when(core == 0)
        def _():
            part_copy(1, u).start()

    @pl.when(core == 1)
    def _():
        pl.semaphore_wait(gate, 1)
        for u in range(2):
            for role in range(2):
                part_copy(role, u).start()

    ahead_valid = inside(place - 2 * sign)
    behind_valid = inside(place + 2 * sign)

    def congruence(slot, middle_of, base_of, store):
        rights = [half_times_adjoint(right_ref, slot, middle_of(h)) for h in range(2)]
        for g in range(2):
            total = base_of(g)
            for h in range(2):
                product = dot(left_ref[slot, g, h], rights[h])
                total = product if total is None else total + product
            store(g, total)

    def store_result(u):
        def store(g, total):
            rows = pl.ds(g * half, half)
            result[u, 0, rows, :] = total[0:half]
            result[u, 1, rows, :] = total[half : 2 * half]

        return store

    for u in range(2):
        local = weight(1, 1 - u) * held[0, 1 - u]
        for b in range(2):
            local = local + weight(2 - sign * (b - u), 1 - core) * held[1, b]
        for role in range(2):
            part_copy(role, u).wait_recv()
        local = local + ahead_valid * partial_in[0, u] + behind_valid * partial_in[1, u]
        held[2, u] = local
        congruence(
            u,
            lambda h, u=u: held[2, u, :, h * half : (h + 1) * half, :],
            lambda g: None,
            store_result(u),
        )

        @pl.when(slab == 0)
        def _():
            for g in range(2):
                chain_copy(u, g).start()

        if u == 0:
            for role in range(2):
                for v in range(2):
                    part_copy(role, v).wait_send()

            @pl.when(core == 0)
            def _():
                pl.semaphore_signal(gate, inc=1, device_id={"slab": slab, "energy": partner}, device_id_type=MESH)

    @pl.when(slab > 0)
    def _():
        def advance(u, carry):
            rights = []
            for h in range(2):
                chain_copy(u, h).wait_recv()
                rights.append(half_times_adjoint(right_ref, 2 + u, incoming[u, :, h * half : (h + 1) * half, :]))
            for g in range(2):
                rows = pl.ds(g * half, half)
                total = jnp.concatenate([result[u, 0, rows, :], result[u, 1, rows, :]], axis=0)
                for h in range(2):
                    total = total + dot(left_ref[2 + u, g, h], rights[h])
                store_result(u)(g, total)

                @pl.when(slab < slabs - 1)
                def _():
                    chain_copy(u, g).start()

            return carry

        lax.fori_loop(0, 2, advance, 0)

    writes = [pltpu.make_async_copy(result.at[u], out_hbm.at[0, u], out_sem.at[u]) for u in range(2)]
    for write in writes:
        write.start()

    @pl.when(slab < slabs - 1)
    def _():
        for u in range(2):
            for g in range(2):
                chain_copy(u, g).wait_send()

    for write in writes:
        write.wait()


def body(retarded, lesser_prev, hopping, hop_mask, offsets, coupling, occupation):
    size = retarded.shape[-1]
    half = size // 2
    any_space = pl.BlockSpec(memory_space=pl.ANY)
    scalars = pl.BlockSpec(memory_space=pltpu.SMEM)
    dma = pltpu.SemaphoreType.DMA
    return pl.pallas_call(
        kernel,
        out_shape=jax.ShapeDtypeStruct(retarded.shape, F32),
        in_specs=[any_space] * 3 + [scalars] * 4,
        out_specs=any_space,
        scratch_shapes=[
            pltpu.VMEM((3, 2, 2, size, size), F32),
            pltpu.VMEM((2, 2, 2, size, size), F32),
            pltpu.VMEM((2, 2, 2, size, size), F32),
            pltpu.VMEM((2, 2, size, size), F32),
            pltpu.VMEM((size, size), F32),
            pltpu.VMEM((2, 2, size, size), F32),
            pltpu.VMEM((2, 2, size, size), F32),
            pltpu.VMEM((4, 6 * size, 2 * size), BF16),
            pltpu.VMEM((4, 2, 2, size, 6 * half), BF16),
            dma((3,)),
            dma((2,)),
            dma((2,)),
            dma((2, 2)),
            dma((2, 2)),
            dma((2, 2)),
            dma((2, 2)),
            dma((2,)),
            pltpu.SemaphoreType.REGULAR,
        ],
        compiler_params=pltpu.CompilerParams(
            collective_id=0, has_side_effects=True, vmem_limit_bytes=60 * 1024 * 1024
        ),
    )(retarded, lesser_prev, hopping, hop_mask, offsets, coupling, occupation)


def solution(mesh):
    return jax.shard_map(
        body,
        mesh=mesh,
        in_specs=(
            P("slab", "energy", None, None, None),
            P("slab", "energy", None, None, None),
            P("slab", None, None),
            P("slab", None, None),
            P(),
            P(),
            P(),
        ),
        out_specs=P("slab", "energy", None, None, None),
        check_vma=False,
    )
```

```python
import jax
import jax.numpy as jnp
from jax import lax
from jax.experimental import pallas as pl
from jax.experimental.pallas import tpu as pltpu
from jax.sharding import PartitionSpec as P

MESH = pl.DeviceIdType.MESH
F32 = jnp.float32
BF16 = jnp.bfloat16
HEAD = 3
CHUNKS = 8


def split(value):
    high = value.astype(BF16)
    return high, (value - high.astype(F32)).astype(BF16)


def dot(left, right):
    return jnp.dot(left, right, preferred_element_type=F32)


def masked_hopping(hop_ref, mask_ref, size):
    tiles = mask_ref.shape[-1]
    tile = size // tiles
    column = lax.broadcasted_iota(jnp.int32, (tile, size), 1)
    rows = []
    for i in range(tiles):
        keep = jnp.full((tile, size), mask_ref[0, i, tiles - 1].astype(F32))
        for j in range(tiles - 2, -1, -1):
            keep = jnp.where(column < (j + 1) * tile, mask_ref[0, i, j].astype(F32), keep)
        rows.append(hop_ref[i * tile : (i + 1) * tile, :] * keep)
    return jnp.concatenate(rows, axis=0)


def prepare(right_ref, left_ref, slot, real, imag):
    size = real.shape[0]
    half = size // 2
    for source, places in ((real, 0), (imag, 1)):
        high, low = split(source.T)
        for part, starts in ((high, (0, 4 * size)), (low, (2 * size,))):
            for start in starts:
                if places == 0:
                    right_ref[slot, start : start + size, 0:size] = part
                    right_ref[slot, start + size : start + 2 * size, size : 2 * size] = part
                else:
                    right_ref[slot, start : start + size, size : 2 * size] = -part
                    right_ref[slot, start + size : start + 2 * size, 0:size] = part
        high, low = split(source)
        for part, starts in ((high, (0, 2 * half)), (low, (4 * half,))):
            for g in range(2):
                for h in range(2):
                    block = part[g * half : (g + 1) * half, h * half : (h + 1) * half]
                    for start in starts:
                        if places == 0:
                            left_ref[slot, g, h, 0:half, start : start + half] = block
                            left_ref[slot, g, h, half : 2 * half, start + half : start + 2 * half] = block
                        else:
                            left_ref[slot, g, h, 0:half, start + half : start + 2 * half] = -block
                            left_ref[slot, g, h, half : 2 * half, start : start + half] = block


def half_times_adjoint(right_ref, slot, middle):
    size = middle.shape[-1]
    real_high, real_low = split(middle[0])
    imag_high, imag_low = split(middle[1])
    left = jnp.concatenate([real_high, imag_high, real_high, imag_high, real_low, imag_low], axis=1)
    product = dot(left, right_ref[slot])
    stacked = jnp.concatenate([product[:, 0:size], product[:, size : 2 * size]], axis=0)
    high, low = split(stacked)
    return jnp.concatenate([high, low, high], axis=0)


def kernel(
    retarded_hbm, lesser_hbm, hop_hbm, mask_ref, offsets_ref, coupling_ref, occupation_ref,
    out_ref,
    held, partial_out, partial_in, retarded, hop, incoming, carried, chained, chained_in,
    right_ref, left_ref,
    load_sem, near_send, near_recv, part_send, part_recv, chain_send, chain_recv, cast_send, cast_recv,
    prod_send, prod_recv, gate, turn,
):
    result = out_ref.at[0]
    slab = lax.axis_index("slab")
    slabs = lax.axis_size("slab")
    place = lax.axis_index("energy")
    places = lax.axis_size("energy")
    core = lax.rem(place, 2)
    sign = 2 * core - 1
    size = retarded.shape[-1]
    half = size // 2
    chunk = size // CHUNKS
    last = slabs - 1

    def ring(index):
        return lax.rem(index + places, places)

    partner = place - sign
    across = ring(place + sign)
    ahead = ring(place + 2 * sign)
    behind = ring(place - 2 * sign)

    def plane(step):
        return lax.rem(slab + step, slabs)

    loads = [
        pltpu.make_async_copy(lesser_hbm.at[0], held.at[0], load_sem.at[0]),
        pltpu.make_async_copy(retarded_hbm.at[0], retarded, load_sem.at[1]),
        pltpu.make_async_copy(hop_hbm.at[0], hop, load_sem.at[2]),
    ]
    for load in loads:
        load.start()

    @pl.when(place - 2 * sign != ring(place - 2 * sign))
    def _():
        partial_in[0] = jnp.zeros_like(partial_in[0])

    @pl.when(place + 2 * sign != ring(place + 2 * sign))
    def _():
        partial_in[1] = jnp.zeros_like(partial_in[1])

    barrier = pltpu.get_barrier_semaphore()
    for other in (partner, across, ahead, behind):
        pl.semaphore_signal(barrier, inc=1, device_id={"slab": slab, "energy": other}, device_id_type=MESH)
    for step in (1, slabs - 1, last - HEAD + 1, slabs - last + HEAD - 1):
        pl.semaphore_signal(barrier, inc=1, device_id={"slab": plane(step), "energy": place}, device_id_type=MESH)
    pl.semaphore_wait(barrier, 8)

    def near_copy(slot, other):
        return pltpu.make_async_remote_copy(
            src_ref=lesser_hbm.at[0], dst_ref=held.at[slot],
            send_sem=near_send.at[slot - 1], recv_sem=near_recv.at[slot - 1],
            device_id={"slab": slab, "energy": other}, device_id_type=MESH,
        )

    to_partner = near_copy(1, partner)
    to_across = near_copy(2, across)
    has_across = (place + sign >= 0) & (place + sign < places)
    has_ahead = (place + 2 * sign >= 0) & (place + 2 * sign < places)
    has_behind = (place - 2 * sign >= 0) & (place - 2 * sign < places)
    to_partner.start()

    @pl.when(has_across)
    def _():
        to_across.start()

    @pl.when(jnp.logical_not(has_across))
    def _():
        held[2] = jnp.zeros_like(held[2])


    def part_copy(role, u, p):
        other = ahead if role == 0 else behind
        return pltpu.make_async_remote_copy(
            src_ref=partial_out.at[role, u, p], dst_ref=partial_in.at[role, u, p],
            send_sem=part_send.at[role, u, p], recv_sem=part_recv.at[role, u, p],
            device_id={"slab": slab, "energy": other}, device_id_type=MESH,
        )

    def slab_copy(source, target, send_sem, recv_sem, to):
        return pltpu.make_async_remote_copy(
            src_ref=source, dst_ref=target, send_sem=send_sem, recv_sem=recv_sem,
            device_id={"slab": to, "energy": place}, device_id_type=MESH,
        )

    def chain_copy(u, g):
        rows = pl.ds(g * half, half)
        return slab_copy(
            result.at[u, :, rows, :], incoming.at[u, :, rows, :], chain_send.at[u, g], chain_recv.at[u, g], plane(1)
        )

    def prod_copy(u, g):
        rows = pl.ds(g * half, half)
        return slab_copy(
            chained.at[u, :, rows, :], chained_in.at[u, :, rows, :], prod_send.at[u, g], prod_recv.at[u, g], plane(1)
        )

    def cast_copy(way, u, c):
        rows = pl.ds(c * chunk, chunk)
        to = HEAD if way == 0 else last
        return slab_copy(
            result.at[u, :, rows, :], carried.at[u, :, rows, :], cast_send.at[way, u, c], cast_recv.at[u, c], to
        )

    def relay_copy(u, c):
        rows = pl.ds(c * chunk, chunk)
        to = jnp.where(slab == HEAD, plane(1), plane(slabs - 1))
        return slab_copy(
            carried.at[u, :, rows, :], carried.at[u, :, rows, :], cast_send.at[0, u, c], cast_recv.at[u, c], to
        )

    first_head = slab == 0
    second_head = slab == HEAD
    is_head = first_head | second_head
    is_caster = slab == HEAD - 1
    chains_on = (slab != HEAD - 1) & (slab != last)
    in_second = slab >= HEAD
    relays = second_head | (slab >= last - 1)

    modes = offsets_ref.shape[0]
    steps = [offsets_ref[k] for k in range(modes)]
    absorb = [coupling_ref[k] * occupation_ref[k] for k in range(modes)]
    emit = [coupling_ref[k] * (occupation_ref[k] + 1.0) for k in range(modes)]

    def weight(distance, above):
        total = jnp.float32(0.0)
        for k in range(modes):
            factor = jnp.where(above == 1, emit[k], absorb[k])
            total = total + jnp.where(steps[k] == distance, factor, 0.0)
        return total

    def hand_over(which):
        pl.semaphore_signal(which, inc=1, device_id={"slab": slab, "energy": partner}, device_id_type=MESH)

    loads[1].wait()
    loads[2].wait()
    mask_high, mask_low = split(masked_hopping(hop, mask_ref, size))
    hopping = jnp.concatenate([mask_high, mask_low, mask_high], axis=0)

    def couple(u, carry):
        real, imag = retarded[u, 0], retarded[u, 1]
        high, low = split(jnp.concatenate([real, imag], axis=0))
        coupled = dot(jnp.concatenate([high, high, low], axis=1), hopping)
        chained[u, 0] = coupled[0:size]
        chained[u, 1] = coupled[size : 2 * size]

        @pl.when(second_head & (core == 0))
        def _():
            for g in range(2):
                prod_copy(u, g).start()

        return carry

    lax.fori_loop(0, 2, couple, 0)

    loads[0].wait()
    to_partner.wait()
    above_ahead = 1 - core
    above_behind = core
    for u in range(2):
        total = None
        for slot, reach in ((0, 4), (1, 6)):
            for b in range(2):
                term = weight(reach + sign * (u - b), above_ahead) * held[slot, b]
                total = term if total is None else total + term
        partial_out[0, u] = total

    @pl.when((core == 0) & has_ahead)
    def _():
        for u in range(2):
            for p in range(2):
                part_copy(0, u, p).start()

    @pl.when((core == 1) & has_ahead)
    def _():
        part_copy(0, 0, 0).start()

    def operands(u, carry):
        prepare(right_ref, left_ref, u, retarded[u, 0], retarded[u, 1])
        prepare(right_ref, left_ref, 2 + u, chained[u, 0], chained[u, 1])
        return carry

    lax.fori_loop(0, 2, operands, 0)

    def products_sent():
        for u in range(2):
            for g in range(2):
                prod_copy(u, g).wait_send()

    def multiply(u):
        rights = []
        for h in range(2):
            prod_copy(u, h).wait_recv()
            rows = pl.ds(h * half, half)
            high, low = split(jnp.concatenate([chained_in[u, 0, rows, :], chained_in[u, 1, rows, :]], axis=0))
            rights.append(jnp.concatenate([high, low, high], axis=0))
        for g in range(2):
            total = dot(left_ref[2 + u, g, 0], rights[0]) + dot(left_ref[2 + u, g, 1], rights[1])
            rows = pl.ds(g * half, half)
            chained[u, 0, rows, :] = total[0:half]
            chained[u, 1, rows, :] = total[half : 2 * half]

        @pl.when(slab < last)
        def _():
            @pl.when((core == 1) & (u == 0))
            def _():
                pl.semaphore_wait(turn.at[0], 1)

            for g in range(2):
                prod_copy(u, g).start()

    early = (slab == HEAD + 1) & (core == 0)

    @pl.when(second_head & (core == 0))
    def _():
        products_sent()
        hand_over(turn.at[0])

    @pl.when(second_head & (core == 1))
    def _():
        pl.semaphore_wait(turn.at[0], 1)
        for u in range(2):
            for g in range(2):
                prod_copy(u, g).start()

    @pl.when(early)
    def _():
        multiply(0)

    @pl.when(has_across)
    def _():
        to_across.wait()

    for u in range(2):
        total = None
        for slot, reach in ((0, 4), (1, 2), (2, 6)):
            for b in range(2):
                factor = weight(reach - sign * (u - b), above_behind)
                term = factor * held[slot, b]
                total = term if total is None else total + term
        partial_out[1, u] = total

        @pl.when((core == 0) & has_behind)
        def _():
            for p in range(2):
                part_copy(1, u, p).start()

    @pl.when(in_second)
    def _():
        def product(u, carry):
            @pl.when((slab > HEAD) & jnp.logical_not(early & (u == 0)))
            def _():
                multiply(u)

            prepare(right_ref, left_ref, 4 + u, chained[u, 0], chained[u, 1])
            return carry

        lax.fori_loop(0, 2, product, 0)

        @pl.when((core == 0) & (slab > HEAD) & (slab < last))
        def _():
            products_sent()
            hand_over(turn.at[0])

    @pl.when(core == 1)
    def _():
        pl.semaphore_wait(gate.at[0], 1)

        @pl.when(has_behind)
        def _():
            for u in range(2):
                for p in range(2):
                    part_copy(1, u, p).start()

        pl.semaphore_wait(gate.at[1], 1)

        @pl.when(has_ahead)
        def _():
            for u in range(2):
                for p in range(2):
                    if u + p > 0:
                        part_copy(0, u, p).start()

    @pl.when((core == 1) & in_second & (slab < last))
    def _():
        products_sent()
        hand_over(turn.at[2])

    def congruence(slot, middle_of, base_of, store):
        rights = [half_times_adjoint(right_ref, slot, middle_of(h)) for h in range(2)]
        for g in range(2):
            total = base_of(g)
            for h in range(2):
                product = dot(left_ref[slot, g, h], rights[h])
                total = product if total is None else total + product
            store(g, total)

    def stacked_result(u, g):
        rows = pl.ds(g * half, half)
        return jnp.concatenate([result[u, 0, rows, :], result[u, 1, rows, :]], axis=0)

    def store_result(u, g, total):
        rows = pl.ds(g * half, half)
        result[u, 0, rows, :] = total[0:half]
        result[u, 1, rows, :] = total[half : 2 * half]

    def send_on(u, g):
        @pl.when(chains_on)
        def _():
            chain_copy(u, g).start()

        @pl.when(is_caster)
        def _():
            for c in range(CHUNKS // 2):
                for way in range(2):
                    cast_copy(way, u, g * (CHUNKS // 2) + c).start()

    def wait_sent():
        @pl.when(chains_on)
        def _():
            for u in range(2):
                for g in range(2):
                    chain_copy(u, g).wait_send()

        @pl.when(is_caster)
        def _():
            for u in range(2):
                for c in range(CHUNKS):
                    for way in range(2):
                        cast_copy(way, u, c).wait_send()

    def parts_sent(role, goes):
        @pl.when(goes)
        def _():
            for v in range(2):
                for p in range(2):
                    part_copy(role, v, p).wait_send()

    def my_turn():
        @pl.when((core == 1) & (slab < last))
        def _():
            pl.semaphore_wait(turn.at[1], 1)

        @pl.when((core == 0) & in_second & (slab < last))
        def _():
            pl.semaphore_wait(turn.at[2], 1)

    def pass_turn():
        @pl.when((core == 0) & (slab < last))
        def _():
            wait_sent()
            hand_over(turn.at[1])

    for u in range(2):
        if u == 0:

            @pl.when(core == 0)
            def _():
                parts_sent(0, has_ahead)
                hand_over(gate.at[0])

        local = weight(1, 1 - u) * held[0, 1 - u]
        for b in range(2):
            local = local + weight(2 - sign * (b - u), 1 - core) * held[1, b]
        for role, comes in ((0, has_behind), (1, has_ahead)):

            @pl.when(comes)
            def _():
                for p in range(2):
                    part_copy(role, u, p).wait_recv()

        local = local + partial_in[0, u] + partial_in[1, u]
        held[2, u] = local
        congruence(
            u,
            lambda h, u=u: held[2, u, :, h * half : (h + 1) * half, :],
            lambda g: None,
            lambda g, total, u=u: store_result(u, g, total),
        )

        if u == 0:

            @pl.when(core == 0)
            def _():
                parts_sent(1, has_behind)
                hand_over(gate.at[1])

        @pl.when(is_head)
        def _():
            if u == 0:
                my_turn()
            for g in range(2):
                send_on(u, g)

        if u == 1:

            @pl.when(is_head)
            def _():
                pass_turn()

    def relay(u):
        for c in range(CHUNKS):
            relay_copy(u, c).wait_recv()
            relay_copy(u, c).start()

    @pl.when(slab == last)
    def _():
        for u in range(2):
            relay(u)

    def advance(u, carry):
        @pl.when(jnp.logical_not(is_head))
        def _():
            rights = []
            for h in range(2):
                chain_copy(u, h).wait_recv()
                rights.append(half_times_adjoint(right_ref, 2 + u, incoming[u, :, h * half : (h + 1) * half, :]))
            for g in range(2):
                total = stacked_result(u, g)
                for h in range(2):
                    total = total + dot(left_ref[2 + u, g, h], rights[h])
                store_result(u, g, total)
                if g == 0:

                    @pl.when(u == 0)
                    def _():
                        my_turn()

                send_on(u, g)

        @pl.when(second_head | (slab == last - 1))
        def _():
            relay(u)

        @pl.when(jnp.logical_not(is_head) & (u == 1))
        def _():
            pass_turn()

        return carry

    lax.fori_loop(0, 2, advance, 0)

    @pl.when(core == 1)
    def _():
        wait_sent()
        parts_sent(0, has_ahead)
        parts_sent(1, has_behind)

    @pl.when(in_second)
    def _():
        def apply(u, carry):
            @pl.when(jnp.logical_not(relays))
            def _():
                for c in range(CHUNKS):
                    relay_copy(u, c).wait_recv()

            congruence(
                4 + u,
                lambda h: carried[u, :, h * half : (h + 1) * half, :],
                lambda g: stacked_result(u, g),
                lambda g, total: store_result(u, g, total),
            )
            return carry

        lax.fori_loop(0, 2, apply, 0)

        @pl.when(relays)
        def _():
            for u in range(2):
                for c in range(CHUNKS):
                    relay_copy(u, c).wait_send()


def body(retarded, lesser_prev, hopping, hop_mask, offsets, coupling, occupation):
    size = retarded.shape[-1]
    half = size // 2
    any_space = pl.BlockSpec(memory_space=pl.ANY)
    scalars = pl.BlockSpec(memory_space=pltpu.SMEM)
    dma = pltpu.SemaphoreType.DMA
    return pl.pallas_call(
        kernel,
        out_shape=pltpu.VMEM(retarded.shape, F32),
        in_specs=[any_space] * 3 + [scalars] * 4,
        out_specs=pl.BlockSpec(memory_space=pltpu.VMEM),
        scratch_shapes=[
            pltpu.VMEM((3, 2, 2, size, size), F32),
            pltpu.VMEM((2, 2, 2, size, size), F32),
            pltpu.VMEM((2, 2, 2, size, size), F32),
            pltpu.VMEM((2, 2, size, size), F32),
            pltpu.VMEM((size, size), F32),
            pltpu.VMEM((2, 2, size, size), F32),
            pltpu.VMEM((2, 2, size, size), F32),
            pltpu.VMEM((2, 2, size, size), F32),
            pltpu.VMEM((2, 2, size, size), F32),
            pltpu.VMEM((6, 6 * size, 2 * size), BF16),
            pltpu.VMEM((6, 2, 2, size, 6 * half), BF16),
            dma((3,)),
            dma((2,)),
            dma((2,)),
            dma((2, 2, 2)),
            dma((2, 2, 2)),
            dma((2, 2)),
            dma((2, 2)),
            dma((2, 2, CHUNKS)),
            dma((2, CHUNKS)),
            dma((2, 2)),
            dma((2, 2)),
            pltpu.SemaphoreType.REGULAR((2,)),
            pltpu.SemaphoreType.REGULAR((3,)),
        ],
        compiler_params=pltpu.CompilerParams(
            collective_id=0, has_side_effects=True, vmem_limit_bytes=60 * 1024 * 1024
        ),
    )(retarded, lesser_prev, hopping, hop_mask, offsets, coupling, occupation)


def solution(mesh):
    return jax.shard_map(
        body,
        mesh=mesh,
        in_specs=(
            P("slab", "energy", None, None, None),
            P("slab", "energy", None, None, None),
            P("slab", None, None),
            P("slab", None, None),
            P(),
            P(),
            P(),
        ),
        out_specs=P("slab", "energy", None, None, None),
        check_vma=False,
    )
```

```python
import jax
import jax.numpy as jnp
from jax import lax
from jax.experimental import pallas as pl
from jax.experimental.pallas import tpu as pltpu
from jax.sharding import PartitionSpec as P

MESH = pl.DeviceIdType.MESH
F32 = jnp.float32
BF16 = jnp.bfloat16
HEAD = 3
CHUNKS = 8


def split(value):
    high = value.astype(BF16)
    return high, (value - high.astype(F32)).astype(BF16)


def dot(left, right):
    return jnp.dot(left, right, preferred_element_type=F32)


def masked_hopping(hop_ref, mask_ref, size):
    tiles = mask_ref.shape[-1]
    tile = size // tiles
    column = lax.broadcasted_iota(jnp.int32, (tile, size), 1)
    rows = []
    for i in range(tiles):
        keep = jnp.full((tile, size), mask_ref[0, i, tiles - 1].astype(F32))
        for j in range(tiles - 2, -1, -1):
            keep = jnp.where(column < (j + 1) * tile, mask_ref[0, i, j].astype(F32), keep)
        rows.append(hop_ref[i * tile : (i + 1) * tile, :] * keep)
    return jnp.concatenate(rows, axis=0)


def prepare(right_ref, left_ref, slot, real, imag):
    size = real.shape[0]
    half = size // 2
    for source, places in ((real, 0), (imag, 1)):
        high, low = split(source.T)
        for part, starts in ((high, (0, 4 * size)), (low, (2 * size,))):
            for start in starts:
                if places == 0:
                    right_ref[slot, start : start + size, 0:size] = part
                    right_ref[slot, start + size : start + 2 * size, size : 2 * size] = part
                else:
                    right_ref[slot, start : start + size, size : 2 * size] = -part
                    right_ref[slot, start + size : start + 2 * size, 0:size] = part
        high, low = split(source)
        for part, starts in ((high, (0, 2 * half)), (low, (4 * half,))):
            for g in range(2):
                for h in range(2):
                    block = part[g * half : (g + 1) * half, h * half : (h + 1) * half]
                    for start in starts:
                        if places == 0:
                            left_ref[slot, g, h, 0:half, start : start + half] = block
                            left_ref[slot, g, h, half : 2 * half, start + half : start + 2 * half] = block
                        else:
                            left_ref[slot, g, h, 0:half, start + half : start + 2 * half] = -block
                            left_ref[slot, g, h, half : 2 * half, start : start + half] = block


def half_times_adjoint(right_ref, slot, middle):
    size = middle.shape[-1]
    real_high, real_low = split(middle[0])
    imag_high, imag_low = split(middle[1])
    left = jnp.concatenate([real_high, imag_high, real_high, imag_high, real_low, imag_low], axis=1)
    product = dot(left, right_ref[slot])
    stacked = jnp.concatenate([product[:, 0:size], product[:, size : 2 * size]], axis=0)
    high, low = split(stacked)
    return jnp.concatenate([high, low, high], axis=0)


def kernel(
    retarded_hbm, lesser_hbm, hop_hbm, mask_ref, offsets_ref, coupling_ref, occupation_ref,
    out_ref,
    held, partial_out, partial_in, retarded, hop, incoming, carried, chained, chained_in,
    right_ref, left_ref,
    load_sem, near_send, near_recv, part_send, part_recv, chain_send, chain_recv, cast_send, cast_recv,
    prod_send, prod_recv, gate, turn,
):
    result = out_ref.at[0]
    slab = lax.axis_index("slab")
    slabs = lax.axis_size("slab")
    place = lax.axis_index("energy")
    places = lax.axis_size("energy")
    core = lax.rem(place, 2)
    sign = 2 * core - 1
    size = retarded.shape[-1]
    half = size // 2
    chunk = size // CHUNKS
    last = slabs - 1

    def ring(index):
        return lax.rem(index + places, places)

    partner = place - sign
    across = ring(place + sign)
    ahead = ring(place + 2 * sign)
    behind = ring(place - 2 * sign)

    def plane(step):
        return lax.rem(slab + step, slabs)

    loads = [
        pltpu.make_async_copy(lesser_hbm.at[0], held.at[0], load_sem.at[0]),
        pltpu.make_async_copy(retarded_hbm.at[0], retarded, load_sem.at[1]),
        pltpu.make_async_copy(hop_hbm.at[0], hop, load_sem.at[2]),
    ]
    for load in loads:
        load.start()

    @pl.when(place - 2 * sign != ring(place - 2 * sign))
    def _():
        partial_in[0] = jnp.zeros_like(partial_in[0])

    @pl.when(place + 2 * sign != ring(place + 2 * sign))
    def _():
        partial_in[1] = jnp.zeros_like(partial_in[1])

    barrier = pltpu.get_barrier_semaphore()
    for other in (partner, across, ahead, behind):
        pl.semaphore_signal(barrier, inc=1, device_id={"slab": slab, "energy": other}, device_id_type=MESH)
    for step in (1, slabs - 1, last - HEAD + 1, slabs - last + HEAD - 1):
        pl.semaphore_signal(barrier, inc=1, device_id={"slab": plane(step), "energy": place}, device_id_type=MESH)
    loads[1].wait()
    loads[2].wait()
    mask_high, mask_low = split(masked_hopping(hop, mask_ref, size))
    hopping = jnp.concatenate([mask_high, mask_low, mask_high], axis=0)

    def couple(u, carry):
        real, imag = retarded[u, 0], retarded[u, 1]
        high, low = split(jnp.concatenate([real, imag], axis=0))
        coupled = dot(jnp.concatenate([high, high, low], axis=1), hopping)
        chained[u, 0] = coupled[0:size]
        chained[u, 1] = coupled[size : 2 * size]

        return carry

    lax.fori_loop(0, 2, couple, 0)

    pl.semaphore_wait(barrier, 8)

    def near_copy(slot, other):
        return pltpu.make_async_remote_copy(
            src_ref=lesser_hbm.at[0], dst_ref=held.at[slot],
            send_sem=near_send.at[slot - 1], recv_sem=near_recv.at[slot - 1],
            device_id={"slab": slab, "energy": other}, device_id_type=MESH,
        )

    to_partner = near_copy(1, partner)
    to_across = near_copy(2, across)
    has_across = (place + sign >= 0) & (place + sign < places)
    has_ahead = (place + 2 * sign >= 0) & (place + 2 * sign < places)
    has_behind = (place - 2 * sign >= 0) & (place - 2 * sign < places)
    to_partner.start()

    @pl.when(has_across)
    def _():
        to_across.start()

    @pl.when(jnp.logical_not(has_across))
    def _():
        held[2] = jnp.zeros_like(held[2])


    def part_copy(role, u, p):
        other = ahead if role == 0 else behind
        return pltpu.make_async_remote_copy(
            src_ref=partial_out.at[role, u, p], dst_ref=partial_in.at[role, u, p],
            send_sem=part_send.at[role, u, p], recv_sem=part_recv.at[role, u, p],
            device_id={"slab": slab, "energy": other}, device_id_type=MESH,
        )

    def slab_copy(source, target, send_sem, recv_sem, to):
        return pltpu.make_async_remote_copy(
            src_ref=source, dst_ref=target, send_sem=send_sem, recv_sem=recv_sem,
            device_id={"slab": to, "energy": place}, device_id_type=MESH,
        )

    def chain_copy(u, g):
        rows = pl.ds(g * half, half)
        return slab_copy(
            result.at[u, :, rows, :], incoming.at[u, :, rows, :], chain_send.at[u, g], chain_recv.at[u, g], plane(1)
        )

    def prod_copy(u, g):
        rows = pl.ds(g * half, half)
        return slab_copy(
            chained.at[u, :, rows, :], chained_in.at[u, :, rows, :], prod_send.at[u, g], prod_recv.at[u, g], plane(1)
        )

    def cast_copy(way, u, c):
        rows = pl.ds(c * chunk, chunk)
        to = HEAD if way == 0 else last
        return slab_copy(
            result.at[u, :, rows, :], carried.at[u, :, rows, :], cast_send.at[way, u, c], cast_recv.at[u, c], to
        )

    def relay_copy(u, c):
        rows = pl.ds(c * chunk, chunk)
        to = jnp.where(slab == HEAD, plane(1), plane(slabs - 1))
        return slab_copy(
            carried.at[u, :, rows, :], carried.at[u, :, rows, :], cast_send.at[0, u, c], cast_recv.at[u, c], to
        )

    first_head = slab == 0
    second_head = slab == HEAD
    is_head = first_head | second_head
    is_caster = slab == HEAD - 1
    chains_on = (slab != HEAD - 1) & (slab != last)
    in_second = slab >= HEAD
    relays = second_head | (slab >= last - 1)

    modes = offsets_ref.shape[0]
    steps = [offsets_ref[k] for k in range(modes)]
    absorb = [coupling_ref[k] * occupation_ref[k] for k in range(modes)]
    emit = [coupling_ref[k] * (occupation_ref[k] + 1.0) for k in range(modes)]

    def weight(distance, above):
        total = jnp.float32(0.0)
        for k in range(modes):
            factor = jnp.where(above == 1, emit[k], absorb[k])
            total = total + jnp.where(steps[k] == distance, factor, 0.0)
        return total

    def hand_over(which):
        pl.semaphore_signal(which, inc=1, device_id={"slab": slab, "energy": partner}, device_id_type=MESH)

    @pl.when(second_head & (core == 0))
    def _():
        for u in range(2):
            for g in range(2):
                prod_copy(u, g).start()

    loads[0].wait()
    to_partner.wait()
    above_ahead = 1 - core
    above_behind = core
    for u in range(2):
        total = None
        for slot, reach in ((0, 4), (1, 6)):
            for b in range(2):
                term = weight(reach + sign * (u - b), above_ahead) * held[slot, b]
                total = term if total is None else total + term
        partial_out[0, u] = total

    @pl.when((core == 0) & has_ahead)
    def _():
        for u in range(2):
            for p in range(2):
                part_copy(0, u, p).start()

    @pl.when((core == 1) & has_ahead)
    def _():
        part_copy(0, 0, 0).start()

    def operands(u, carry):
        prepare(right_ref, left_ref, u, retarded[u, 0], retarded[u, 1])
        prepare(right_ref, left_ref, 2 + u, chained[u, 0], chained[u, 1])
        return carry

    lax.fori_loop(0, 2, operands, 0)

    def products_sent(which):
        for u in range(2):
            for g in range(2):
                prod_copy(u, g).wait_send()
        hand_over(which)

    def multiply(u):
        rights = []
        for h in range(2):
            prod_copy(u, h).wait_recv()
            rows = pl.ds(h * half, half)
            high, low = split(jnp.concatenate([chained_in[u, 0, rows, :], chained_in[u, 1, rows, :]], axis=0))
            rights.append(jnp.concatenate([high, low, high], axis=0))
        for g in range(2):
            total = dot(left_ref[2 + u, g, 0], rights[0]) + dot(left_ref[2 + u, g, 1], rights[1])
            rows = pl.ds(g * half, half)
            chained[u, 0, rows, :] = total[0:half]
            chained[u, 1, rows, :] = total[half : 2 * half]

        @pl.when(slab < last)
        def _():
            @pl.when((core == 1) & (u == 0))
            def _():
                pl.semaphore_wait(turn.at[0], 1)

            for g in range(2):
                prod_copy(u, g).start()

    early = (slab == HEAD + 1) & (core == 0)

    @pl.when(second_head & (core == 0))
    def _():
        products_sent(turn.at[0])

    @pl.when(second_head & (core == 1))
    def _():
        pl.semaphore_wait(turn.at[0], 1)
        for u in range(2):
            for g in range(2):
                prod_copy(u, g).start()

    @pl.when(early)
    def _():
        multiply(0)

    @pl.when(has_across)
    def _():
        to_across.wait()

    for u in range(2):
        total = None
        for slot, reach in ((0, 4), (1, 2), (2, 6)):
            for b in range(2):
                factor = weight(reach - sign * (u - b), above_behind)
                term = factor * held[slot, b]
                total = term if total is None else total + term
        partial_out[1, u] = total

        @pl.when((core == 0) & has_behind)
        def _():
            for p in range(2):
                part_copy(1, u, p).start()

    @pl.when(in_second)
    def _():
        def product(u, carry):
            @pl.when((slab > HEAD) & jnp.logical_not(early & (u == 0)))
            def _():
                multiply(u)

            prepare(right_ref, left_ref, 4 + u, chained[u, 0], chained[u, 1])
            return carry

        lax.fori_loop(0, 2, product, 0)

        @pl.when((core == 0) & (slab > HEAD) & (slab < last))
        def _():
            products_sent(turn.at[0])

    @pl.when(core == 1)
    def _():
        pl.semaphore_wait(gate.at[0], 1)

        @pl.when(has_behind)
        def _():
            for u in range(2):
                for p in range(2):
                    part_copy(1, u, p).start()

        @pl.when(in_second & (slab < last))
        def _():
            products_sent(turn.at[2])

        pl.semaphore_wait(gate.at[1], 1)

        @pl.when(has_ahead)
        def _():
            for u in range(2):
                for p in range(2):
                    if u + p > 0:
                        part_copy(0, u, p).start()

    def congruence(slot, middle_of, base_of, store):
        rights = [half_times_adjoint(right_ref, slot, middle_of(h)) for h in range(2)]
        for g in range(2):
            total = base_of(g)
            for h in range(2):
                product = dot(left_ref[slot, g, h], rights[h])
                total = product if total is None else total + product
            store(g, total)

    def stacked_result(u, g):
        rows = pl.ds(g * half, half)
        return jnp.concatenate([result[u, 0, rows, :], result[u, 1, rows, :]], axis=0)

    def store_result(u, g, total):
        rows = pl.ds(g * half, half)
        result[u, 0, rows, :] = total[0:half]
        result[u, 1, rows, :] = total[half : 2 * half]

    def send_on(u, g):
        @pl.when(chains_on)
        def _():
            chain_copy(u, g).start()

        @pl.when(is_caster)
        def _():
            for c in range(CHUNKS // 2):
                for way in range(2):
                    cast_copy(way, u, g * (CHUNKS // 2) + c).start()

    def wait_sent():
        @pl.when(chains_on)
        def _():
            for u in range(2):
                for g in range(2):
                    chain_copy(u, g).wait_send()

        @pl.when(is_caster)
        def _():
            for u in range(2):
                for c in range(CHUNKS):
                    for way in range(2):
                        cast_copy(way, u, c).wait_send()

    def parts_sent(role, goes):
        @pl.when(goes)
        def _():
            for v in range(2):
                for p in range(2):
                    part_copy(role, v, p).wait_send()

    def my_turn():
        @pl.when((core == 1) & (slab < last))
        def _():
            pl.semaphore_wait(turn.at[1], 1)

        @pl.when((core == 0) & in_second & (slab < last))
        def _():
            pl.semaphore_wait(turn.at[2], 1)

    def pass_turn():
        @pl.when((core == 0) & (slab < last))
        def _():
            wait_sent()
            hand_over(turn.at[1])

    def relay(u):
        for c in range(CHUNKS):
            relay_copy(u, c).wait_recv()
            relay_copy(u, c).start()

    late = (slab == last) & (core == 1)
    for u in range(2):

        @pl.when(late)
        def _():
            relay(u)

        local = weight(1, 1 - u) * held[0, 1 - u]
        for b in range(2):
            local = local + weight(2 - sign * (b - u), 1 - core) * held[1, b]
        for role, comes in ((0, has_behind), (1, has_ahead)):

            @pl.when(comes)
            def _():
                for p in range(2):
                    part_copy(role, u, p).wait_recv()

        local = local + partial_in[0, u] + partial_in[1, u]
        held[2, u] = local
        congruence(
            u,
            lambda h, u=u: held[2, u, :, h * half : (h + 1) * half, :],
            lambda g: None,
            lambda g, total, u=u: store_result(u, g, total),
        )

        def start(u=u):
            if u == 0:
                my_turn()
            for g in range(2):
                send_on(u, g)

        pl.when(first_head)(start)
        if u == 0:

            @pl.when(core == 0)
            def _():
                parts_sent(0, has_ahead)
                hand_over(gate.at[0])
                parts_sent(1, has_behind)
                hand_over(gate.at[1])

        pl.when(second_head)(start)
        if u == 1:

            @pl.when(is_head)
            def _():
                pass_turn()

            @pl.when(second_head & (core == 1))
            def _():
                wait_sent()
                hand_over(turn.at[3])

            @pl.when(second_head & (core == 0))
            def _():
                pl.semaphore_wait(turn.at[3], 1)

    def apply(u):
        congruence(
            4 + u,
            lambda h: carried[u, :, h * half : (h + 1) * half, :],
            lambda g: stacked_result(u, g),
            lambda g, total: store_result(u, g, total),
        )

    @pl.when(slab == last)
    def _():
        def pass_and_use(u, carry):
            @pl.when(jnp.logical_not(late))
            def _():
                relay(u)

            apply(u)
            return carry

        lax.fori_loop(0, 2, pass_and_use, 0)

    def advance(u, carry):
        @pl.when(jnp.logical_not(is_head))
        def _():
            rights = []
            for h in range(2):
                chain_copy(u, h).wait_recv()
                rights.append(half_times_adjoint(right_ref, 2 + u, incoming[u, :, h * half : (h + 1) * half, :]))
            for g in range(2):
                total = stacked_result(u, g)
                for h in range(2):
                    total = total + dot(left_ref[2 + u, g, h], rights[h])
                store_result(u, g, total)
                if g == 0:

                    @pl.when(u == 0)
                    def _():
                        my_turn()

                send_on(u, g)

        @pl.when(second_head | (slab == last - 1))
        def _():
            relay(u)

        @pl.when(jnp.logical_not(is_head) & (u == 1))
        def _():
            pass_turn()

        return carry

    lax.fori_loop(0, 2, advance, 0)

    @pl.when((core == 1) & jnp.logical_not(second_head))
    def _():
        wait_sent()

    @pl.when(core == 1)
    def _():
        parts_sent(0, has_ahead)
        parts_sent(1, has_behind)

    @pl.when(in_second & (slab < last))
    def _():
        def use(u, carry):
            @pl.when(jnp.logical_not(relays))
            def _():
                for c in range(CHUNKS):
                    relay_copy(u, c).wait_recv()

            apply(u)
            return carry

        lax.fori_loop(0, 2, use, 0)

    @pl.when(relays)
    def _():
        for u in range(2):
            for c in range(CHUNKS):
                relay_copy(u, c).wait_send()


def body(retarded, lesser_prev, hopping, hop_mask, offsets, coupling, occupation):
    size = retarded.shape[-1]
    half = size // 2
    any_space = pl.BlockSpec(memory_space=pl.ANY)
    scalars = pl.BlockSpec(memory_space=pltpu.SMEM)
    dma = pltpu.SemaphoreType.DMA
    return pl.pallas_call(
        kernel,
        out_shape=pltpu.VMEM(retarded.shape, F32),
        in_specs=[any_space] * 3 + [scalars] * 4,
        out_specs=pl.BlockSpec(memory_space=pltpu.VMEM),
        scratch_shapes=[
            pltpu.VMEM((3, 2, 2, size, size), F32),
            pltpu.VMEM((2, 2, 2, size, size), F32),
            pltpu.VMEM((2, 2, 2, size, size), F32),
            pltpu.VMEM((2, 2, size, size), F32),
            pltpu.VMEM((size, size), F32),
            pltpu.VMEM((2, 2, size, size), F32),
            pltpu.VMEM((2, 2, size, size), F32),
            pltpu.VMEM((2, 2, size, size), F32),
            pltpu.VMEM((2, 2, size, size), F32),
            pltpu.VMEM((6, 6 * size, 2 * size), BF16),
            pltpu.VMEM((6, 2, 2, size, 6 * half), BF16),
            dma((3,)),
            dma((2,)),
            dma((2,)),
            dma((2, 2, 2)),
            dma((2, 2, 2)),
            dma((2, 2)),
            dma((2, 2)),
            dma((2, 2, CHUNKS)),
            dma((2, CHUNKS)),
            dma((2, 2)),
            dma((2, 2)),
            pltpu.SemaphoreType.REGULAR((2,)),
            pltpu.SemaphoreType.REGULAR((4,)),
        ],
        compiler_params=pltpu.CompilerParams(
            collective_id=0, has_side_effects=True, vmem_limit_bytes=60 * 1024 * 1024
        ),
    )(retarded, lesser_prev, hopping, hop_mask, offsets, coupling, occupation)


def solution(mesh):
    return jax.shard_map(
        body,
        mesh=mesh,
        in_specs=(
            P("slab", "energy", None, None, None),
            P("slab", "energy", None, None, None),
            P("slab", None, None),
            P("slab", None, None),
            P(),
            P(),
            P(),
        ),
        out_specs=P("slab", "energy", None, None, None),
        check_vma=False,
    )
```

```python
import jax
import jax.numpy as jnp
from jax import lax
from jax.experimental import pallas as pl
from jax.experimental.pallas import tpu as pltpu
from jax.sharding import PartitionSpec as P

MESH = pl.DeviceIdType.MESH
F32 = jnp.float32
BF16 = jnp.bfloat16
HEAD = 3
CHUNKS = 8


def split(value):
    high = value.astype(BF16)
    return high, (value - high.astype(F32)).astype(BF16)


def dot(left, right):
    return jnp.dot(left, right, preferred_element_type=F32)


def masked_hopping(hop_ref, mask_ref, size):
    tiles = mask_ref.shape[-1]
    tile = size // tiles
    column = lax.broadcasted_iota(jnp.int32, (tile, size), 1)
    rows = []
    for i in range(tiles):
        keep = jnp.full((tile, size), mask_ref[0, i, tiles - 1].astype(F32))
        for j in range(tiles - 2, -1, -1):
            keep = jnp.where(column < (j + 1) * tile, mask_ref[0, i, j].astype(F32), keep)
        rows.append(hop_ref[i * tile : (i + 1) * tile, :] * keep)
    return jnp.concatenate(rows, axis=0)


def prepare(right_ref, left_ref, slot, real, imag):
    size = real.shape[0]
    half = size // 2
    for source, places in ((real, 0), (imag, 1)):
        high, low = split(source.T)
        for part, starts in ((high, (0, 4 * size)), (low, (2 * size,))):
            for start in starts:
                if places == 0:
                    right_ref[slot, start : start + size, 0:size] = part
                    right_ref[slot, start + size : start + 2 * size, size : 2 * size] = part
                else:
                    right_ref[slot, start : start + size, size : 2 * size] = -part
                    right_ref[slot, start + size : start + 2 * size, 0:size] = part
        high, low = split(source)
        for part, starts in ((high, (0, 2 * half)), (low, (4 * half,))):
            for g in range(2):
                for h in range(2):
                    block = part[g * half : (g + 1) * half, h * half : (h + 1) * half]
                    for start in starts:
                        if places == 0:
                            left_ref[slot, g, h, 0:half, start : start + half] = block
                            left_ref[slot, g, h, half : 2 * half, start + half : start + 2 * half] = block
                        else:
                            left_ref[slot, g, h, 0:half, start + half : start + 2 * half] = -block
                            left_ref[slot, g, h, half : 2 * half, start : start + half] = block


def half_times_adjoint(right_ref, slot, middle):
    size = middle.shape[-1]
    real_high, real_low = split(middle[0])
    imag_high, imag_low = split(middle[1])
    left = jnp.concatenate([real_high, imag_high, real_high, imag_high, real_low, imag_low], axis=1)
    product = dot(left, right_ref[slot])
    stacked = jnp.concatenate([product[:, 0:size], product[:, size : 2 * size]], axis=0)
    high, low = split(stacked)
    return jnp.concatenate([high, low, high], axis=0)


def kernel(
    retarded_hbm, lesser_hbm, hop_hbm, mask_ref, offsets_ref, coupling_ref, occupation_ref,
    out_ref,
    held, partial_out, partial_in, retarded, hop, incoming, carried, chained, chained_in,
    right_ref, left_ref,
    load_sem, near_send, near_recv, part_send, part_recv, chain_send, chain_recv, cast_send, cast_recv,
    prod_send, prod_recv, gate, turn,
):
    result = out_ref.at[0]
    slab = lax.axis_index("slab")
    slabs = lax.axis_size("slab")
    place = lax.axis_index("energy")
    places = lax.axis_size("energy")
    core = lax.rem(place, 2)
    sign = 2 * core - 1
    size = retarded.shape[-1]
    half = size // 2
    chunk = size // CHUNKS
    last = slabs - 1

    def ring(index):
        return lax.rem(index + places, places)

    partner = place - sign
    across = ring(place + sign)
    ahead = ring(place + 2 * sign)
    behind = ring(place - 2 * sign)

    def plane(step):
        return lax.rem(slab + step, slabs)

    loads = [
        pltpu.make_async_copy(lesser_hbm.at[0], held.at[0], load_sem.at[0]),
        pltpu.make_async_copy(retarded_hbm.at[0], retarded, load_sem.at[1]),
        pltpu.make_async_copy(hop_hbm.at[0], hop, load_sem.at[2]),
    ]
    for load in loads:
        load.start()

    @pl.when(place - 2 * sign != ring(place - 2 * sign))
    def _():
        partial_in[0] = jnp.zeros_like(partial_in[0])

    @pl.when(place + 2 * sign != ring(place + 2 * sign))
    def _():
        partial_in[1] = jnp.zeros_like(partial_in[1])

    barrier = pltpu.get_barrier_semaphore()
    for other in (partner, across, ahead, behind):
        pl.semaphore_signal(barrier, inc=1, device_id={"slab": slab, "energy": other}, device_id_type=MESH)
    for step in (1, slabs - 1, last - HEAD + 1, slabs - last + HEAD - 1):
        pl.semaphore_signal(barrier, inc=1, device_id={"slab": plane(step), "energy": place}, device_id_type=MESH)
    loads[1].wait()
    loads[2].wait()
    mask_high, mask_low = split(masked_hopping(hop, mask_ref, size))
    hopping = jnp.concatenate([mask_high, mask_low, mask_high], axis=0)

    def couple(u, carry):
        real, imag = retarded[u, 0], retarded[u, 1]
        high, low = split(jnp.concatenate([real, imag], axis=0))
        coupled = dot(jnp.concatenate([high, high, low], axis=1), hopping)
        chained[u, 0] = coupled[0:size]
        chained[u, 1] = coupled[size : 2 * size]

        return carry

    lax.fori_loop(0, 2, couple, 0)

    pl.semaphore_wait(barrier, 8)

    def near_copy(slot, other):
        return pltpu.make_async_remote_copy(
            src_ref=lesser_hbm.at[0], dst_ref=held.at[slot],
            send_sem=near_send.at[slot - 1], recv_sem=near_recv.at[slot - 1],
            device_id={"slab": slab, "energy": other}, device_id_type=MESH,
        )

    to_partner = near_copy(1, partner)
    to_across = near_copy(2, across)
    has_across = (place + sign >= 0) & (place + sign < places)
    has_ahead = (place + 2 * sign >= 0) & (place + 2 * sign < places)
    has_behind = (place - 2 * sign >= 0) & (place - 2 * sign < places)
    to_partner.start()

    @pl.when(has_across)
    def _():
        to_across.start()

    @pl.when(jnp.logical_not(has_across))
    def _():
        held[2] = jnp.zeros_like(held[2])


    def part_copy(role, u, p):
        other = ahead if role == 0 else behind
        return pltpu.make_async_remote_copy(
            src_ref=partial_out.at[role, u, p], dst_ref=partial_in.at[role, u, p],
            send_sem=part_send.at[role, u, p], recv_sem=part_recv.at[role, u, p],
            device_id={"slab": slab, "energy": other}, device_id_type=MESH,
        )

    def slab_copy(source, target, send_sem, recv_sem, to):
        return pltpu.make_async_remote_copy(
            src_ref=source, dst_ref=target, send_sem=send_sem, recv_sem=recv_sem,
            device_id={"slab": to, "energy": place}, device_id_type=MESH,
        )

    def rows_of(k):
        return pl.ds(0, half) if k == 0 else pl.ds(half + (k - 1) * (half // 2), half // 2)

    def pieces_of(g):
        return (0,) if g == 0 else (1, 2)

    def chain_copy(u, k):
        rows = rows_of(k)
        return slab_copy(
            result.at[u, :, rows, :], incoming.at[u, :, rows, :], chain_send.at[u, k], chain_recv.at[u, k], plane(1)
        )

    def prod_copy(u, k):
        rows = rows_of(k)
        return slab_copy(
            chained.at[u, :, rows, :], chained_in.at[u, :, rows, :], prod_send.at[u, k], prod_recv.at[u, k], plane(1)
        )

    def cast_copy(way, u, c):
        rows = pl.ds(c * chunk, chunk)
        to = HEAD if way == 0 else last
        return slab_copy(
            result.at[u, :, rows, :], carried.at[u, :, rows, :], cast_send.at[way, u, c], cast_recv.at[u, c], to
        )

    def relay_copy(u, c):
        rows = pl.ds(c * chunk, chunk)
        to = jnp.where(slab == HEAD, plane(1), plane(slabs - 1))
        return slab_copy(
            carried.at[u, :, rows, :], carried.at[u, :, rows, :], cast_send.at[0, u, c], cast_recv.at[u, c], to
        )

    first_head = slab == 0
    second_head = slab == HEAD
    is_head = first_head | second_head
    is_caster = slab == HEAD - 1
    chains_on = (slab != HEAD - 1) & (slab != last)
    in_second = slab >= HEAD
    relays = second_head | (slab >= last - 1)

    modes = offsets_ref.shape[0]
    steps = [offsets_ref[k] for k in range(modes)]
    absorb = [coupling_ref[k] * occupation_ref[k] for k in range(modes)]
    emit = [coupling_ref[k] * (occupation_ref[k] + 1.0) for k in range(modes)]

    def weight(distance, above):
        total = jnp.float32(0.0)
        for k in range(modes):
            factor = jnp.where(above == 1, emit[k], absorb[k])
            total = total + jnp.where(steps[k] == distance, factor, 0.0)
        return total

    def hand_over(which):
        pl.semaphore_signal(which, inc=1, device_id={"slab": slab, "energy": partner}, device_id_type=MESH)

    @pl.when(second_head & (core == 0))
    def _():
        for u in range(2):
            for k in range(3):
                prod_copy(u, k).start()

    loads[0].wait()
    to_partner.wait()
    above_ahead = 1 - core
    above_behind = core
    for u in range(2):
        total = None
        for slot, reach in ((0, 4), (1, 6)):
            for b in range(2):
                term = weight(reach + sign * (u - b), above_ahead) * held[slot, b]
                total = term if total is None else total + term
        partial_out[0, u] = total

    @pl.when((core == 0) & has_ahead)
    def _():
        for u in range(2):
            for p in range(2):
                part_copy(0, u, p).start()

    @pl.when((core == 1) & has_ahead)
    def _():
        part_copy(0, 0, 0).start()

    def operands(u, carry):
        prepare(right_ref, left_ref, u, retarded[u, 0], retarded[u, 1])
        prepare(right_ref, left_ref, 2 + u, chained[u, 0], chained[u, 1])
        return carry

    lax.fori_loop(0, 2, operands, 0)

    def products_sent(which):
        for u in range(2):
            for k in range(3 - u):
                prod_copy(u, k).wait_send()
        hand_over(which)
        prod_copy(1, 2).wait_send()

    def multiply(u):
        rights = []
        for h in range(2):
            for k in pieces_of(h):
                prod_copy(u, k).wait_recv()
            rows = pl.ds(h * half, half)
            high, low = split(jnp.concatenate([chained_in[u, 0, rows, :], chained_in[u, 1, rows, :]], axis=0))
            rights.append(jnp.concatenate([high, low, high], axis=0))
        for g in range(2):
            total = dot(left_ref[2 + u, g, 0], rights[0]) + dot(left_ref[2 + u, g, 1], rights[1])
            rows = pl.ds(g * half, half)
            chained[u, 0, rows, :] = total[0:half]
            chained[u, 1, rows, :] = total[half : 2 * half]

        @pl.when(slab < last)
        def _():
            @pl.when((core == 1) & (u == 0))
            def _():
                pl.semaphore_wait(turn.at[0], 1)

            for k in range(3):
                prod_copy(u, k).start()

    early = (slab == HEAD + 1) & (core == 0)

    @pl.when(second_head & (core == 0))
    def _():
        products_sent(turn.at[0])

    @pl.when(second_head & (core == 1))
    def _():
        pl.semaphore_wait(turn.at[0], 1)
        for u in range(2):
            for k in range(3):
                prod_copy(u, k).start()

    @pl.when(early)
    def _():
        multiply(0)

    @pl.when(has_across)
    def _():
        to_across.wait()

    for u in range(2):
        total = None
        for slot, reach in ((0, 4), (1, 2), (2, 6)):
            for b in range(2):
                factor = weight(reach - sign * (u - b), above_behind)
                term = factor * held[slot, b]
                total = term if total is None else total + term
        partial_out[1, u] = total

        @pl.when((core == 0) & has_behind)
        def _():
            for p in range(2):
                part_copy(1, u, p).start()

    @pl.when(in_second)
    def _():
        def product(u, carry):
            @pl.when((slab > HEAD) & jnp.logical_not(early & (u == 0)))
            def _():
                multiply(u)

            prepare(right_ref, left_ref, 4 + u, chained[u, 0], chained[u, 1])
            return carry

        lax.fori_loop(0, 2, product, 0)

        @pl.when((core == 0) & (slab > HEAD) & (slab < last))
        def _():
            products_sent(turn.at[0])

    @pl.when(core == 1)
    def _():
        pl.semaphore_wait(gate.at[0], 1)

        @pl.when(has_behind)
        def _():
            for u in range(2):
                for p in range(2):
                    part_copy(1, u, p).start()

        @pl.when(second_head)
        def _():
            products_sent(turn.at[2])

        pl.semaphore_wait(gate.at[1], 1)

        @pl.when(has_ahead)
        def _():
            for u in range(2):
                for p in range(2):
                    if u + p > 0:
                        part_copy(0, u, p).start()

        @pl.when((slab > HEAD) & (slab < last))
        def _():
            products_sent(turn.at[2])

    def congruence(slot, middle_of, base_of, store):
        rights = [half_times_adjoint(right_ref, slot, middle_of(h)) for h in range(2)]
        for g in range(2):
            total = base_of(g)
            for h in range(2):
                product = dot(left_ref[slot, g, h], rights[h])
                total = product if total is None else total + product
            store(g, total)

    def stacked_result(u, g):
        rows = pl.ds(g * half, half)
        return jnp.concatenate([result[u, 0, rows, :], result[u, 1, rows, :]], axis=0)

    def store_result(u, g, total):
        rows = pl.ds(g * half, half)
        result[u, 0, rows, :] = total[0:half]
        result[u, 1, rows, :] = total[half : 2 * half]

    def send_on(u, g):
        @pl.when(chains_on)
        def _():
            for k in pieces_of(g):
                chain_copy(u, k).start()

        @pl.when(is_caster)
        def _():
            for c in range(CHUNKS // 2):
                for way in range(2):
                    cast_copy(way, u, g * (CHUNKS // 2) + c).start()

    def wait_sent(which=None):
        @pl.when(chains_on)
        def _():
            for u in range(2):
                for k in range(3 - u):
                    chain_copy(u, k).wait_send()

        @pl.when(is_caster)
        def _():
            for u in range(2):
                for c in range(CHUNKS - 2 * u):
                    for way in range(2):
                        cast_copy(way, u, c).wait_send()

        if which is not None:
            hand_over(which)

        @pl.when(chains_on)
        def _():
            chain_copy(1, 2).wait_send()

        @pl.when(is_caster)
        def _():
            for c in range(CHUNKS - 2, CHUNKS):
                for way in range(2):
                    cast_copy(way, 1, c).wait_send()

    def parts_sent(role, goes):
        @pl.when(goes)
        def _():
            for v in range(2):
                for p in range(2):
                    part_copy(role, v, p).wait_send()

    def my_turn():
        @pl.when((core == 1) & (slab < last))
        def _():
            pl.semaphore_wait(turn.at[1], 1)

        @pl.when((core == 0) & in_second & (slab < last))
        def _():
            pl.semaphore_wait(turn.at[2], 1)

    def pass_turn():
        @pl.when((core == 0) & (slab < last))
        def _():
            wait_sent(turn.at[1])

    def relay(u, first=0, end=CHUNKS):
        for c in range(first, end):
            relay_copy(u, c).wait_recv()
            relay_copy(u, c).start()

    late = (slab == last) & (core == 1)
    for u in range(2):

        @pl.when(late)
        def _():
            relay(u)

        local = weight(1, 1 - u) * held[0, 1 - u]
        for b in range(2):
            local = local + weight(2 - sign * (b - u), 1 - core) * held[1, b]
        for role, comes in ((0, has_behind), (1, has_ahead)):

            @pl.when(comes)
            def _():
                for p in range(2):
                    part_copy(role, u, p).wait_recv()

        local = local + partial_in[0, u] + partial_in[1, u]
        held[2, u] = local
        congruence(
            u,
            lambda h, u=u: held[2, u, :, h * half : (h + 1) * half, :],
            lambda g: None,
            lambda g, total, u=u: store_result(u, g, total),
        )

        def start(u=u):
            if u == 0:
                my_turn()
            for g in range(2):
                send_on(u, g)

        pl.when(first_head)(start)
        if u == 0:

            @pl.when(core == 0)
            def _():
                parts_sent(0, has_ahead)
                hand_over(gate.at[0])

        pl.when(second_head)(start)
        if u == 0:

            @pl.when(core == 0)
            def _():
                parts_sent(1, has_behind)
                hand_over(gate.at[1])

        if u == 1:

            @pl.when(is_head)
            def _():
                pass_turn()

            @pl.when(second_head & (core == 1))
            def _():
                wait_sent(turn.at[3])

            @pl.when(second_head & (core == 0))
            def _():
                pl.semaphore_wait(turn.at[3], 1)

    def apply(u):
        congruence(
            4 + u,
            lambda h: carried[u, :, h * half : (h + 1) * half, :],
            lambda g: stacked_result(u, g),
            lambda g, total: store_result(u, g, total),
        )

    @pl.when(slab == last)
    def _():
        def pass_and_use(u, carry):
            @pl.when(jnp.logical_not(late))
            def _():
                relay(u)

            apply(u)
            return carry

        lax.fori_loop(0, 2, pass_and_use, 0)

    def advance(u, carry):
        @pl.when(jnp.logical_not(is_head))
        def _():
            for h in range(2):
                for k in pieces_of(h):
                    chain_copy(u, k).wait_recv()
                right = half_times_adjoint(right_ref, 2 + u, incoming[u, :, h * half : (h + 1) * half, :])
                for g in range(2):
                    store_result(u, g, stacked_result(u, g) + dot(left_ref[2 + u, g, h], right))
                    if h == 1:
                        if g == 0:

                            @pl.when(u == 0)
                            def _():
                                my_turn()

                        send_on(u, g)
                if h == 0:

                    @pl.when(slab == last - 1)
                    def _():
                        relay(u, 0, CHUNKS // 2)


        @pl.when(second_head)
        def _():
            relay(u)

        @pl.when(slab == last - 1)
        def _():
            relay(u, CHUNKS // 2)

        @pl.when(jnp.logical_not(is_head) & (u == 1))
        def _():
            pass_turn()

        return carry

    lax.fori_loop(0, 2, advance, 0)

    @pl.when((core == 1) & jnp.logical_not(second_head))
    def _():
        wait_sent()

    @pl.when(core == 1)
    def _():
        parts_sent(0, has_ahead)
        parts_sent(1, has_behind)

    @pl.when(in_second & (slab < last))
    def _():
        def use(u, carry):
            @pl.when(jnp.logical_not(relays))
            def _():
                for c in range(CHUNKS):
                    relay_copy(u, c).wait_recv()

            apply(u)
            return carry

        lax.fori_loop(0, 2, use, 0)

    @pl.when(relays)
    def _():
        for u in range(2):
            for c in range(CHUNKS):
                relay_copy(u, c).wait_send()


def body(retarded, lesser_prev, hopping, hop_mask, offsets, coupling, occupation):
    size = retarded.shape[-1]
    half = size // 2
    any_space = pl.BlockSpec(memory_space=pl.ANY)
    scalars = pl.BlockSpec(memory_space=pltpu.SMEM)
    dma = pltpu.SemaphoreType.DMA
    return pl.pallas_call(
        kernel,
        out_shape=pltpu.VMEM(retarded.shape, F32),
        in_specs=[any_space] * 3 + [scalars] * 4,
        out_specs=pl.BlockSpec(memory_space=pltpu.VMEM),
        scratch_shapes=[
            pltpu.VMEM((3, 2, 2, size, size), F32),
            pltpu.VMEM((2, 2, 2, size, size), F32),
            pltpu.VMEM((2, 2, 2, size, size), F32),
            pltpu.VMEM((2, 2, size, size), F32),
            pltpu.VMEM((size, size), F32),
            pltpu.VMEM((2, 2, size, size), F32),
            pltpu.VMEM((2, 2, size, size), F32),
            pltpu.VMEM((2, 2, size, size), F32),
            pltpu.VMEM((2, 2, size, size), F32),
            pltpu.VMEM((6, 6 * size, 2 * size), BF16),
            pltpu.VMEM((6, 2, 2, size, 6 * half), BF16),
            dma((3,)),
            dma((2,)),
            dma((2,)),
            dma((2, 2, 2)),
            dma((2, 2, 2)),
            dma((2, 3)),
            dma((2, 3)),
            dma((2, 2, CHUNKS)),
            dma((2, CHUNKS)),
            dma((2, 3)),
            dma((2, 3)),
            pltpu.SemaphoreType.REGULAR((2,)),
            pltpu.SemaphoreType.REGULAR((4,)),
        ],
        compiler_params=pltpu.CompilerParams(
            collective_id=0, has_side_effects=True, vmem_limit_bytes=60 * 1024 * 1024
        ),
    )(retarded, lesser_prev, hopping, hop_mask, offsets, coupling, occupation)


def solution(mesh):
    return jax.shard_map(
        body,
        mesh=mesh,
        in_specs=(
            P("slab", "energy", None, None, None),
            P("slab", "energy", None, None, None),
            P("slab", None, None),
            P("slab", None, None),
            P(),
            P(),
            P(),
        ),
        out_specs=P("slab", "energy", None, None, None),
        check_vma=False,
    )
```

```python
import jax
import jax.numpy as jnp
from jax import lax
from jax.experimental import pallas as pl
from jax.experimental.pallas import tpu as pltpu
from jax.sharding import PartitionSpec as P

MESH = pl.DeviceIdType.MESH
F32 = jnp.float32
BF16 = jnp.bfloat16
HEAD = 3
CHUNKS = 8


def split(value):
    high = value.astype(BF16)
    return high, (value - high.astype(F32)).astype(BF16)


def dot(left, right):
    return jnp.dot(left, right, preferred_element_type=F32)


def masked_hopping(hop_ref, mask_ref, size):
    tiles = mask_ref.shape[-1]
    tile = size // tiles
    column = lax.broadcasted_iota(jnp.int32, (tile, size), 1)
    rows = []
    for i in range(tiles):
        keep = jnp.full((tile, size), mask_ref[0, i, tiles - 1].astype(F32))
        for j in range(tiles - 2, -1, -1):
            keep = jnp.where(column < (j + 1) * tile, mask_ref[0, i, j].astype(F32), keep)
        rows.append(hop_ref[i * tile : (i + 1) * tile, :] * keep)
    return jnp.concatenate(rows, axis=0)


def prepare(right_ref, left_ref, slot, real, imag):
    size = real.shape[0]
    half = size // 2
    for source, places in ((real, 0), (imag, 1)):
        high, low = split(source.T)
        for part, starts in ((high, (0, 4 * size)), (low, (2 * size,))):
            for start in starts:
                if places == 0:
                    right_ref[slot, start : start + size, 0:size] = part
                    right_ref[slot, start + size : start + 2 * size, size : 2 * size] = part
                else:
                    right_ref[slot, start : start + size, size : 2 * size] = -part
                    right_ref[slot, start + size : start + 2 * size, 0:size] = part
        high, low = split(source)
        for part, starts in ((high, (0, 2 * half)), (low, (4 * half,))):
            for g in range(2):
                for h in range(2):
                    block = part[g * half : (g + 1) * half, h * half : (h + 1) * half]
                    for start in starts:
                        if places == 0:
                            left_ref[slot, g, h, 0:half, start : start + half] = block
                            left_ref[slot, g, h, half : 2 * half, start + half : start + 2 * half] = block
                        else:
                            left_ref[slot, g, h, 0:half, start + half : start + 2 * half] = -block
                            left_ref[slot, g, h, half : 2 * half, start : start + half] = block


def half_times_adjoint(right_ref, slot, middle):
    size = middle.shape[-1]
    real_high, real_low = split(middle[0])
    imag_high, imag_low = split(middle[1])
    left = jnp.concatenate([real_high, imag_high, real_high, imag_high, real_low, imag_low], axis=1)
    product = dot(left, right_ref[slot])
    stacked = jnp.concatenate([product[:, 0:size], product[:, size : 2 * size]], axis=0)
    high, low = split(stacked)
    return jnp.concatenate([high, low, high], axis=0)


def kernel(
    retarded_hbm, lesser_hbm, hop_hbm, mask_ref, offsets_ref, coupling_ref, occupation_ref,
    out_ref,
    held, partial_out, partial_in, retarded, hop, incoming, carried, chained, chained_in,
    right_ref, left_ref,
    load_sem, near_send, near_recv, part_send, part_recv, chain_send, chain_recv, cast_send, cast_recv,
    prod_send, prod_recv, gate, turn,
):
    result = out_ref.at[0]
    slab = lax.axis_index("slab")
    slabs = lax.axis_size("slab")
    place = lax.axis_index("energy")
    places = lax.axis_size("energy")
    core = lax.rem(place, 2)
    sign = 2 * core - 1
    size = retarded.shape[-1]
    half = size // 2
    chunk = size // CHUNKS
    last = slabs - 1

    def ring(index):
        return lax.rem(index + places, places)

    partner = place - sign
    across = ring(place + sign)
    ahead = ring(place + 2 * sign)
    behind = ring(place - 2 * sign)

    def plane(step):
        return lax.rem(slab + step, slabs)

    loads = [
        pltpu.make_async_copy(lesser_hbm.at[0], held.at[0], load_sem.at[0]),
        pltpu.make_async_copy(retarded_hbm.at[0], retarded, load_sem.at[1]),
        pltpu.make_async_copy(hop_hbm.at[0], hop, load_sem.at[2]),
    ]
    for load in loads:
        load.start()

    @pl.when(place - 2 * sign != ring(place - 2 * sign))
    def _():
        partial_in[0] = jnp.zeros_like(partial_in[0])

    @pl.when(place + 2 * sign != ring(place + 2 * sign))
    def _():
        partial_in[1] = jnp.zeros_like(partial_in[1])

    barrier = pltpu.get_barrier_semaphore()
    for other in (partner, across, ahead, behind):
        pl.semaphore_signal(barrier, inc=1, device_id={"slab": slab, "energy": other}, device_id_type=MESH)
    for step in (1, slabs - 1, last - HEAD + 1, slabs - last + HEAD - 1):
        pl.semaphore_signal(barrier, inc=1, device_id={"slab": plane(step), "energy": place}, device_id_type=MESH)
    loads[1].wait()
    loads[2].wait()
    mask_high, mask_low = split(masked_hopping(hop, mask_ref, size))
    hopping = jnp.concatenate([mask_high, mask_low, mask_high], axis=0)

    def couple(u, carry):
        real, imag = retarded[u, 0], retarded[u, 1]
        high, low = split(jnp.concatenate([real, imag], axis=0))
        coupled = dot(jnp.concatenate([high, high, low], axis=1), hopping)
        chained[u, 0] = coupled[0:size]
        chained[u, 1] = coupled[size : 2 * size]

        return carry

    lax.fori_loop(0, 2, couple, 0)

    pl.semaphore_wait(barrier, 8)

    def near_copy(slot, other):
        return pltpu.make_async_remote_copy(
            src_ref=lesser_hbm.at[0], dst_ref=held.at[slot],
            send_sem=near_send.at[slot - 1], recv_sem=near_recv.at[slot - 1],
            device_id={"slab": slab, "energy": other}, device_id_type=MESH,
        )

    to_partner = near_copy(1, partner)
    to_across = near_copy(2, across)
    has_across = (place + sign >= 0) & (place + sign < places)
    has_ahead = (place + 2 * sign >= 0) & (place + 2 * sign < places)
    has_behind = (place - 2 * sign >= 0) & (place - 2 * sign < places)
    to_partner.start()

    @pl.when(has_across)
    def _():
        to_across.start()

    @pl.when(jnp.logical_not(has_across))
    def _():
        held[2] = jnp.zeros_like(held[2])


    def part_copy(role, u, p):
        other = ahead if role == 0 else behind
        return pltpu.make_async_remote_copy(
            src_ref=partial_out.at[role, u, p], dst_ref=partial_in.at[role, u, p],
            send_sem=part_send.at[role, u, p], recv_sem=part_recv.at[role, u, p],
            device_id={"slab": slab, "energy": other}, device_id_type=MESH,
        )

    def slab_copy(source, target, send_sem, recv_sem, to):
        return pltpu.make_async_remote_copy(
            src_ref=source, dst_ref=target, send_sem=send_sem, recv_sem=recv_sem,
            device_id={"slab": to, "energy": place}, device_id_type=MESH,
        )

    def rows_of(k):
        return (pl.ds(0, half), pl.ds(half, half * 3 // 4), pl.ds(half + half * 3 // 4, half // 4))[k]

    def pieces_of(g):
        return (0,) if g == 0 else (1, 2)

    def chain_copy(u, k):
        rows = rows_of(k)
        return slab_copy(
            result.at[u, :, rows, :], incoming.at[u, :, rows, :], chain_send.at[u, k], chain_recv.at[u, k], plane(1)
        )

    def prod_copy(u, k):
        rows = rows_of(k)
        return slab_copy(
            chained.at[u, :, rows, :], chained_in.at[u, :, rows, :], prod_send.at[u, k], prod_recv.at[u, k], plane(1)
        )

    def cast_copy(way, u, c):
        rows = pl.ds(c * chunk, chunk)
        to = HEAD if way == 0 else last
        return slab_copy(
            result.at[u, :, rows, :], carried.at[u, :, rows, :], cast_send.at[way, u, c], cast_recv.at[u, c], to
        )

    def relay_copy(u, c):
        rows = pl.ds(c * chunk, chunk)
        to = jnp.where(slab == HEAD, plane(1), plane(slabs - 1))
        return slab_copy(
            carried.at[u, :, rows, :], carried.at[u, :, rows, :], cast_send.at[0, u, c], cast_recv.at[u, c], to
        )

    first_head = slab == 0
    second_head = slab == HEAD
    is_head = first_head | second_head
    is_caster = slab == HEAD - 1
    chains_on = (slab != HEAD - 1) & (slab != last)
    in_second = slab >= HEAD
    relays = second_head | (slab >= last - 1)

    modes = offsets_ref.shape[0]
    steps = [offsets_ref[k] for k in range(modes)]
    absorb = [coupling_ref[k] * occupation_ref[k] for k in range(modes)]
    emit = [coupling_ref[k] * (occupation_ref[k] + 1.0) for k in range(modes)]

    def weight(distance, above):
        total = jnp.float32(0.0)
        for k in range(modes):
            factor = jnp.where(above == 1, emit[k], absorb[k])
            total = total + jnp.where(steps[k] == distance, factor, 0.0)
        return total

    def hand_over(which):
        pl.semaphore_signal(which, inc=1, device_id={"slab": slab, "energy": partner}, device_id_type=MESH)

    @pl.when(second_head & (core == 0))
    def _():
        for u in range(2):
            for k in range(3):
                prod_copy(u, k).start()

    loads[0].wait()
    to_partner.wait()
    above_ahead = 1 - core
    above_behind = core
    for u in range(2):
        total = None
        for slot, reach in ((0, 4), (1, 6)):
            for b in range(2):
                term = weight(reach + sign * (u - b), above_ahead) * held[slot, b]
                total = term if total is None else total + term
        partial_out[0, u] = total

    @pl.when((core == 0) & has_ahead)
    def _():
        for u in range(2):
            for p in range(2):
                part_copy(0, u, p).start()

    @pl.when((core == 1) & has_ahead)
    def _():
        part_copy(0, 0, 0).start()

    def operands(u, carry):
        prepare(right_ref, left_ref, u, retarded[u, 0], retarded[u, 1])
        prepare(right_ref, left_ref, 2 + u, chained[u, 0], chained[u, 1])
        return carry

    lax.fori_loop(0, 2, operands, 0)

    def products_sent(which):
        for u in range(2):
            for k in range(3 - u):
                prod_copy(u, k).wait_send()
        hand_over(which)
        prod_copy(1, 2).wait_send()

    def multiply(u):
        rights = []
        for h in range(2):
            for k in pieces_of(h):
                prod_copy(u, k).wait_recv()
            rows = pl.ds(h * half, half)
            high, low = split(jnp.concatenate([chained_in[u, 0, rows, :], chained_in[u, 1, rows, :]], axis=0))
            rights.append(jnp.concatenate([high, low, high], axis=0))
        for g in range(2):
            total = dot(left_ref[2 + u, g, 0], rights[0]) + dot(left_ref[2 + u, g, 1], rights[1])
            rows = pl.ds(g * half, half)
            chained[u, 0, rows, :] = total[0:half]
            chained[u, 1, rows, :] = total[half : 2 * half]

        @pl.when(slab < last)
        def _():
            @pl.when((core == 1) & (u == 0))
            def _():
                pl.semaphore_wait(turn.at[0], 1)

            for k in range(3):
                prod_copy(u, k).start()

    early = (slab == HEAD + 1) & (core == 0)

    @pl.when(second_head & (core == 0))
    def _():
        products_sent(turn.at[0])

    @pl.when(second_head & (core == 1))
    def _():
        pl.semaphore_wait(turn.at[0], 1)
        for u in range(2):
            for k in range(3):
                prod_copy(u, k).start()

    @pl.when(early)
    def _():
        multiply(0)

    @pl.when(has_across)
    def _():
        to_across.wait()

    @pl.when(place == 1)
    def _():
        hand_over(turn.at[4])

    @pl.when(place == 0)
    def _():
        pl.semaphore_wait(turn.at[4], 1)

    for u in range(2):
        total = None
        for slot, reach in ((0, 4), (1, 2), (2, 6)):
            for b in range(2):
                factor = weight(reach - sign * (u - b), above_behind)
                term = factor * held[slot, b]
                total = term if total is None else total + term
        partial_out[1, u] = total

        @pl.when((core == 0) & has_behind)
        def _():
            for p in range(2):
                part_copy(1, u, p).start()

    @pl.when(in_second)
    def _():
        def product(u, carry):
            @pl.when((slab > HEAD) & jnp.logical_not(early & (u == 0)))
            def _():
                multiply(u)

            prepare(right_ref, left_ref, 4 + u, chained[u, 0], chained[u, 1])
            return carry

        lax.fori_loop(0, 2, product, 0)

        @pl.when((core == 0) & (slab > HEAD) & (slab < last))
        def _():
            products_sent(turn.at[0])

    @pl.when(core == 1)
    def _():
        pl.semaphore_wait(gate.at[0], 1)

        @pl.when(has_behind)
        def _():
            for u in range(2):
                for p in range(2):
                    part_copy(1, u, p).start()

        @pl.when(second_head)
        def _():
            products_sent(turn.at[2])

        pl.semaphore_wait(gate.at[1], 1)

        @pl.when(has_ahead)
        def _():
            for u in range(2):
                for p in range(2):
                    if u + p > 0:
                        part_copy(0, u, p).start()

        @pl.when((slab > HEAD) & (slab < last))
        def _():
            products_sent(turn.at[2])

    def congruence(slot, middle_of, base_of, store):
        rights = [half_times_adjoint(right_ref, slot, middle_of(h)) for h in range(2)]
        for g in range(2):
            total = base_of(g)
            for h in range(2):
                product = dot(left_ref[slot, g, h], rights[h])
                total = product if total is None else total + product
            store(g, total)

    def stacked_result(u, g):
        rows = pl.ds(g * half, half)
        return jnp.concatenate([result[u, 0, rows, :], result[u, 1, rows, :]], axis=0)

    def store_result(u, g, total):
        rows = pl.ds(g * half, half)
        result[u, 0, rows, :] = total[0:half]
        result[u, 1, rows, :] = total[half : 2 * half]

    def send_on(u, g):
        @pl.when(chains_on)
        def _():
            for k in pieces_of(g):
                chain_copy(u, k).start()

        @pl.when(is_caster)
        def _():
            for c in range(CHUNKS // 2):
                for way in range(2):
                    cast_copy(way, u, g * (CHUNKS // 2) + c).start()

    def wait_sent(which=None):
        @pl.when(chains_on)
        def _():
            for u in range(2):
                for k in range(3 - u):
                    chain_copy(u, k).wait_send()

        @pl.when(is_caster)
        def _():
            for u in range(2):
                for c in range(CHUNKS - 2 * u):
                    for way in range(2):
                        cast_copy(way, u, c).wait_send()

        if which is not None:
            hand_over(which)

        @pl.when(chains_on)
        def _():
            chain_copy(1, 2).wait_send()

        @pl.when(is_caster)
        def _():
            for c in range(CHUNKS - 2, CHUNKS):
                for way in range(2):
                    cast_copy(way, 1, c).wait_send()

    def parts_sent(role, goes):
        @pl.when(goes)
        def _():
            for v in range(2):
                for p in range(2):
                    part_copy(role, v, p).wait_send()

    def my_turn():
        @pl.when((core == 1) & (slab < last))
        def _():
            pl.semaphore_wait(turn.at[1], 1)

        @pl.when((core == 0) & in_second & (slab < last))
        def _():
            pl.semaphore_wait(turn.at[2], 1)

    def pass_turn():
        @pl.when((core == 0) & (slab < last))
        def _():
            wait_sent(turn.at[1])

    def relay(u, first=0, end=CHUNKS):
        for c in range(first, end):
            relay_copy(u, c).wait_recv()
            relay_copy(u, c).start()

    late = (slab == last) & (core == 1)
    for u in range(2):

        @pl.when(late)
        def _():
            relay(u)

        local = weight(1, 1 - u) * held[0, 1 - u]
        for b in range(2):
            local = local + weight(2 - sign * (b - u), 1 - core) * held[1, b]
        for role, comes in ((0, has_behind), (1, has_ahead)):

            @pl.when(comes)
            def _():
                for p in range(2):
                    part_copy(role, u, p).wait_recv()

        local = local + partial_in[0, u] + partial_in[1, u]
        held[2, u] = local
        congruence(
            u,
            lambda h, u=u: held[2, u, :, h * half : (h + 1) * half, :],
            lambda g: None,
            lambda g, total, u=u: store_result(u, g, total),
        )

        def start(u=u):
            if u == 0:
                my_turn()
            for g in range(2):
                send_on(u, g)

        pl.when(first_head)(start)
        if u == 0:

            @pl.when(core == 0)
            def _():
                parts_sent(0, has_ahead)
                hand_over(gate.at[0])

        pl.when(second_head)(start)
        if u == 0:

            @pl.when(core == 0)
            def _():
                parts_sent(1, has_behind)
                hand_over(gate.at[1])

        if u == 1:

            @pl.when(is_head)
            def _():
                pass_turn()

            @pl.when(second_head & (core == 1))
            def _():
                wait_sent(turn.at[3])

            @pl.when(second_head & (core == 0))
            def _():
                pl.semaphore_wait(turn.at[3], 1)

    def apply(u):
        congruence(
            4 + u,
            lambda h: carried[u, :, h * half : (h + 1) * half, :],
            lambda g: stacked_result(u, g),
            lambda g, total: store_result(u, g, total),
        )

    @pl.when(slab == last)
    def _():
        def pass_and_use(u, carry):
            @pl.when(jnp.logical_not(late))
            def _():
                relay(u)

            apply(u)
            return carry

        lax.fori_loop(0, 2, pass_and_use, 0)

    def advance(u, carry):
        @pl.when(jnp.logical_not(is_head))
        def _():
            for h in range(2):
                for k in pieces_of(h):
                    chain_copy(u, k).wait_recv()
                right = half_times_adjoint(right_ref, 2 + u, incoming[u, :, h * half : (h + 1) * half, :])
                for g in range(2):
                    store_result(u, g, stacked_result(u, g) + dot(left_ref[2 + u, g, h], right))
                    if h == 1:
                        if g == 0:

                            @pl.when(u == 0)
                            def _():
                                my_turn()

                        send_on(u, g)
                if h == 0:

                    @pl.when(slab == last - 1)
                    def _():
                        relay(u, 0, CHUNKS // 2)


        @pl.when(second_head)
        def _():
            relay(u)

        @pl.when(slab == last - 1)
        def _():
            relay(u, CHUNKS // 2)

        @pl.when(jnp.logical_not(is_head) & (u == 1))
        def _():
            pass_turn()

        return carry

    lax.fori_loop(0, 2, advance, 0)

    @pl.when((core == 1) & jnp.logical_not(in_second))
    def _():
        wait_sent()

    @pl.when(core == 1)
    def _():
        parts_sent(0, has_ahead)
        parts_sent(1, has_behind)

    @pl.when(in_second & (slab < last))
    def _():
        def use(u, carry):
            @pl.when((core == 1) & jnp.logical_not(second_head))
            def _():
                for k in range(3):
                    chain_copy(u, k).wait_send()

            @pl.when(jnp.logical_not(relays))
            def _():
                for c in range(CHUNKS):
                    relay_copy(u, c).wait_recv()

            apply(u)
            return carry

        lax.fori_loop(0, 2, use, 0)

    @pl.when(relays)
    def _():
        for u in range(2):
            for c in range(CHUNKS):
                relay_copy(u, c).wait_send()


def body(retarded, lesser_prev, hopping, hop_mask, offsets, coupling, occupation):
    size = retarded.shape[-1]
    half = size // 2
    any_space = pl.BlockSpec(memory_space=pl.ANY)
    scalars = pl.BlockSpec(memory_space=pltpu.SMEM)
    dma = pltpu.SemaphoreType.DMA
    return pl.pallas_call(
        kernel,
        out_shape=pltpu.VMEM(retarded.shape, F32),
        in_specs=[any_space] * 3 + [scalars] * 4,
        out_specs=pl.BlockSpec(memory_space=pltpu.VMEM),
        scratch_shapes=[
            pltpu.VMEM((3, 2, 2, size, size), F32),
            pltpu.VMEM((2, 2, 2, size, size), F32),
            pltpu.VMEM((2, 2, 2, size, size), F32),
            pltpu.VMEM((2, 2, size, size), F32),
            pltpu.VMEM((size, size), F32),
            pltpu.VMEM((2, 2, size, size), F32),
            pltpu.VMEM((2, 2, size, size), F32),
            pltpu.VMEM((2, 2, size, size), F32),
            pltpu.VMEM((2, 2, size, size), F32),
            pltpu.VMEM((6, 6 * size, 2 * size), BF16),
            pltpu.VMEM((6, 2, 2, size, 6 * half), BF16),
            dma((3,)),
            dma((2,)),
            dma((2,)),
            dma((2, 2, 2)),
            dma((2, 2, 2)),
            dma((2, 3)),
            dma((2, 3)),
            dma((2, 2, CHUNKS)),
            dma((2, CHUNKS)),
            dma((2, 3)),
            dma((2, 3)),
            pltpu.SemaphoreType.REGULAR((2,)),
            pltpu.SemaphoreType.REGULAR((5,)),
        ],
        compiler_params=pltpu.CompilerParams(
            collective_id=0, has_side_effects=True, vmem_limit_bytes=60 * 1024 * 1024
        ),
    )(retarded, lesser_prev, hopping, hop_mask, offsets, coupling, occupation)


def solution(mesh):
    return jax.shard_map(
        body,
        mesh=mesh,
        in_specs=(
            P("slab", "energy", None, None, None),
            P("slab", "energy", None, None, None),
            P("slab", None, None),
            P("slab", None, None),
            P(),
            P(),
            P(),
        ),
        out_specs=P("slab", "energy", None, None, None),
        check_vma=False,
    )
```
